256 devices in a mesh: member: 8 (over z), cell: 32 (over x, y, core).
Axes of the slice: x: 4, y: 4, z: 8, core: 2. Of those that a mesh axis runs over, the one named last changes fastest.
Arguments:
- prior: float32 [64, 524288], P('member', 'cell')
- samples: float32 [64, 524288], P('member', 'cell')
- noise: float32 [2, 64, 524288], P(None, 'member', 'cell'), may hold values from -6 to 6
- obs_cells: int32 [2, 65536], P(None, 'cell'), may hold values from 0 to 524287, as said below
- obs_values: float32 [2, 65536], P(None, 'cell'), may hold values from -6 to 6
- seismic_mask: int32 [2, 4096], P(None, 'cell'), may hold values 0 or 1
Outputs:
- analysis: float32 [64, 524288], P('member', 'cell')
The draws below stay inside these ranges and needn't reach their ends.
Inputs may be any that keep to these rules, and one draw needn't show every extreme that they name: obs_cells[s, o] lies in cells k * 16384 to (k + 1) * 16384 - 1 where k = o // 2048; cells may repeat.
All inputs are finite; a program needn't handle non-finite values. No bound on the sum of `seismic_mask` on one device may be relied on, other than what follows from the above.
Results may differ from the reference program's by a relative error of at most 0.0003.
Values sent between devices are 32-bit elements; how exact they have to be, the bound alone decides.
No kernel may reach another device: no remote copies, remote signals or barrier semaphores. Data moves between devices by JAX's collectives and lax.ppermute only.
A program may use at most 64 MiB of HBM per device.

```python
import math
import jax
import jax.numpy as jnp
from jax import lax

ENS = 64
C_DEV = 16384
SURVEYS = 2
STEPS = 2
NCELLS = 524288
OBS_DEV = 2048
OBS = 65536


def draw_prior(key, part):
    first, second = jax.random.split(key)
    where = jnp.arange(NCELLS, dtype=jnp.float32) / NCELLS
    rough = jax.random.uniform(first, (NCELLS,), jnp.float32, 0.7, 1.4)
    scale = 0.6 * jnp.exp(where * math.log(3.0)) * rough
    base = jax.random.normal(second, (ENS, NCELLS), jnp.float32)
    return base * scale[None, :]


def draw_samples(key, part):
    first = jax.random.fold_in(key, 0)
    base = jax.random.normal(first, (ENS, NCELLS), jnp.float32)
    return jnp.clip(base, -6.0, 6.0)


def draw_obs_cells(key, part):
    local = jax.random.randint(key, (SURVEYS, OBS), 0, C_DEV, dtype=jnp.int32)
    block = jnp.arange(OBS, dtype=jnp.int32) // OBS_DEV
    cells = local + block[None, :] * C_DEV
    cells = cells.at[0, 0].set(0)
    cells = cells.at[0, OBS - 1].set(NCELLS - 1)
    return cells


def plant(values, rng, low, top_value):
    extent = values.shape
    place = [jax.random.randint(jax.random.fold_in(rng, axis), (), 0, extent[axis]) for axis in range(len(extent))]
    values = values.at[tuple(place)].set(low)
    longest = extent.index(max(extent))
    place[longest] = (place[longest] + 1) % extent[longest]
    return values.at[tuple(place)].set(top_value)


def level_of(key, shape, shards, least, largest):
    level, own = 1.0, jax.random.fold_in(key, 6)
    for axis_at, parts in shards:
        steps = jnp.exp(jax.random.uniform(jax.random.fold_in(own, axis_at), (parts,), jnp.float32, least / len(shards), largest / len(shards)))
        level = level * jnp.repeat(steps, shape[axis_at] // parts).reshape([-1 if axis == axis_at else 1 for axis in range(len(shape))])
    return level


def scatter_about(rng, dims, deviation, bound, cuts=(), kind=jnp.bfloat16):
    values = jax.random.normal(rng, dims, jnp.float32) * deviation
    if len(cuts) > 0:
        values = level_of(rng, dims, cuts, -0.22, 0.18) * values
    return jnp.clip(values, min=-bound, max=bound).astype(kind)


def setup_inputs(seed: int = 0) -> dict:
    keys = jax.random.split(jax.random.key(seed), 7)
    return {
        "prior": draw_prior(jax.random.fold_in(keys[6], 71), 0),
        "samples": draw_samples(jax.random.fold_in(keys[6], 71), 0),
        "noise": scatter_about(keys[2], (STEPS, ENS, NCELLS), 1.0, 6.0, ((1, 8), (2, 32)), jnp.float32),
        "obs_cells": draw_obs_cells(jax.random.fold_in(keys[6], 71), 0),
        "obs_values": scatter_about(keys[4], (SURVEYS, OBS), 1.0, 6.0, ((1, 32),), jnp.float32),
        "seismic_mask": plant((jax.random.randint(keys[5], (SURVEYS, NCELLS // 128), 0, 4) < 3).astype(jnp.int32), jax.random.fold_in(keys[5], 1), 0, 1),
    }


def reference(prior, samples, noise, obs_cells, obs_values, seismic_mask):
    ncell = prior.shape[1]
    precision_field = jnp.zeros((ncell,), jnp.float32)
    target_field = jnp.zeros((ncell,), jnp.float32)
    for survey in range(obs_cells.shape[0]):
        where = obs_cells[survey].astype(jnp.int32)
        flags = seismic_mask[survey].astype(jnp.float32)
        weight = flags[where // 128]
        precision_field = precision_field.at[where].add(weight)
        target_field = target_field.at[where].add(weight * obs_values[survey])
    prior_sq = lax.optimization_barrier(jnp.sum(prior * prior, axis=1))
    state = samples
    for step in range(STEPS):
        time_now = 0.6 - 0.1 * step
        alpha = 1.0 - 0.95 * time_now
        beta2 = time_now
        drift = -0.95 / alpha
        diffusion = 1.0 - 2.0 * drift * beta2
        cross = lax.dot_general(state, prior, (((1,), (1,)), ((), ())), precision=lax.Precision.HIGHEST, preferred_element_type=jnp.float32)
        dist = alpha * alpha * prior_sq[None, :] - 2.0 * alpha * cross
        weights = jax.nn.softmax(-dist / (2.0 * beta2 * math.sqrt(ncell)), axis=1)
        mean = jnp.dot(weights, prior, precision=lax.Precision.HIGHEST, preferred_element_type=jnp.float32)
        score = (alpha * mean - state) / beta2 - (1.0 - time_now) * (precision_field[None, :] * state - target_field[None, :])
        state = state - 0.1 * (drift * state - diffusion * score) + math.sqrt(0.1 * diffusion) * noise[step]
    return state
```

```python
import math

import jax
import jax.numpy as jnp
from jax import lax
from jax.experimental import pallas as pl
from jax.experimental.pallas import tpu as pltpu
from jax.sharding import PartitionSpec as P

STEPS = 2
RINGS = 8
ROWS = 8
BF = jnp.bfloat16
F32 = jnp.float32
NT = (((1,), (1,)), ((), ()))
NN = (((1,), (0,)), ((), ()))


def constants(step):
    t = 0.6 - 0.1 * step
    alpha = 1.0 - 0.95 * t
    drift = -0.95 / alpha
    diffusion = 1.0 - 2.0 * drift * t
    return dict(
        t=t,
        alpha=alpha,
        gain=1.0 - 0.1 * drift - 0.1 * diffusion / t,
        pull=0.1 * diffusion * (1.0 - t),
        lift=0.1 * diffusion * alpha / t,
        kick=math.sqrt(0.1 * diffusion),
    )


def split3(x):
    a = x.astype(BF).astype(F32)
    r = x - a
    b = r.astype(BF).astype(F32)
    return a, b, r - b


def prep_kernel(cells, vals, mask, samples, noise, u_ref, base_ref, ab_ref, prec, targ):
    width = prec.shape[0]
    obs = cells.shape[1]
    rows = lax.broadcasted_iota(jnp.int32, (width, obs), 0)
    eye = lax.broadcasted_iota(jnp.int32, (width, width), 0) == lax.broadcasted_iota(
        jnp.int32, (width, width), 1
    )
    p_sum = jnp.zeros((width, width), F32)
    t_sum = jnp.zeros((width, width), F32)
    for s in range(cells.shape[0]):
        local = cells[s : s + 1, :] & (width * width - 1)
        high = jnp.where(rows == (local >> 7), 1.0, 0.0).astype(BF)
        low = rows == (local & 127)
        pieces = [jnp.ones((1, obs), F32), *split3(vals[s : s + 1, :])]
        sums = [
            lax.dot_general(
                high, jnp.where(low, piece, 0.0).astype(BF), NT, preferred_element_type=F32
            )
            for piece in pieces
        ]
        flags = mask[s : s + 1, :].astype(F32)
        flags = jnp.sum(jnp.where(eye, flags, 0.0), axis=1, keepdims=True)
        p_sum += flags * sums[0]
        t_sum += flags * (sums[1] + sums[2] + sums[3])
    prec[...] = p_sum
    targ[...] = t_sum
    k0, k1 = constants(0), constants(1)

    def body(h, carry):
        where = pl.ds(pl.multiple_of(h * width, width), width)
        p = prec[pl.ds(h, 1), :]
        t = targ[pl.ds(h, 1), :]
        u = (
            (k0["gain"] - k0["pull"] * p) * samples[:, where]
            + k0["pull"] * t
            + k0["kick"] * noise[0, :, where]
        )
        a1 = k1["gain"] - k1["pull"] * p
        u_ref[:, where] = u
        base_ref[:, where] = a1 * u + k1["pull"] * t + k1["kick"] * noise[1, :, where]
        ab_ref[:, where] = jnp.broadcast_to(k0["lift"] * a1, (ROWS, width))
        return carry

    lax.fori_loop(0, width, body, 0, unroll=4)


def prep(cells, vals, mask, samples, noise):
    shape = jax.ShapeDtypeStruct(samples.shape, F32)
    return pl.pallas_call(
        prep_kernel,
        out_shape=(shape, shape, shape),
        scratch_shapes=[pltpu.VMEM((128, 128), F32), pltpu.VMEM((128, 128), F32)],
        cost_estimate=pl.CostEstimate(flops=10**9, bytes_accessed=4 * 10**6, transcendentals=0),
        name="prep",
    )(cells, vals, mask, samples, noise)


CHUNK = 1024


def products(lhs, rhs):
    halves = len(lhs[0])
    acc = None
    for half in range(halves):
        left = [x[half] for x in lhs]
        right = [x[half] for x in rhs]

        def body(i, acc, left=left, right=right):
            where = pl.ds(pl.multiple_of(i * CHUNK, CHUNK), CHUNK)
            a = jnp.concatenate([x[:, where] for x in left], axis=0)
            b = jnp.concatenate([x[:, where] for x in right], axis=0)
            a = jnp.concatenate(split3(a), axis=0).astype(BF)
            b = jnp.concatenate(split3(b), axis=0).astype(BF)
            return acc + lax.dot_general(a, b, NT, preferred_element_type=F32)

        if acc is None:
            acc = jnp.zeros((3 * ROWS * len(lhs), 3 * ROWS * len(rhs)), F32)
        acc = lax.fori_loop(0, left[0].shape[1] // CHUNK, body, acc)
    m, n = ROWS * len(lhs), ROWS * len(rhs)
    acc = acc[:m] + acc[m : 2 * m] + acc[2 * m :]
    return acc[:, :n] + acc[:, n : 2 * n] + acc[:, 2 * n :]


def pieces_of(full):
    half = full.shape[1] // 2
    return [full.at[:, :half], full.at[:, half:]]


def gram_kernel(samples, u, own, *refs):
    blocks, out = refs[:-1], refs[-1]
    blocks = [blocks[i : i + 2] for i in range(0, len(blocks), 2)]
    p = [pieces_of(own), *blocks]
    out[...] = products([pieces_of(samples), pieces_of(u), *p], p)


def last_kernel(samples, u, own, *refs):
    blocks, early, out = refs[:-2], refs[-2], refs[-1]
    blocks = [blocks[i : i + 2] for i in range(0, len(blocks), 2)]
    p = [pieces_of(own), *blocks]
    last = products([pieces_of(samples), pieces_of(u), *p], p[-1:])
    m, n = early.shape
    out[:m, :n] = early[...]
    out[:, n:] = last
    out[m:, :n] = last[2 * ROWS : m, :].T


def gram(kernel, shape, *args):
    return pl.pallas_call(
        kernel,
        out_shape=jax.ShapeDtypeStruct(shape, F32),
        cost_estimate=pl.CostEstimate(flops=10**9, bytes_accessed=4 * 10**6, transcendentals=0),
        name=kernel.__name__,
    )(*args)


def softmax(x):
    e = jnp.exp(x - jnp.max(x, axis=1, keepdims=True))
    return e / jnp.sum(e, axis=1, keepdims=True)


def final_kernel(ncell, z, base, ab, own, *refs):
    blocks, out = refs[:-1], refs[-1]
    blocks = [pieces_of(own), *[blocks[i : i + 2] for i in range(0, len(blocks), 2)]]
    n = z.shape[1]
    k0, k1 = constants(0), constants(1)
    pp = z[2 * ROWS :, :]
    eye = lax.broadcasted_iota(jnp.int32, (n, n), 0) == lax.broadcasted_iota(jnp.int32, (n, n), 1)
    norm = jnp.sum(jnp.where(eye, pp, 0.0), axis=0, keepdims=True)

    def weights(k, cross):
        dist = k["alpha"] * k["alpha"] * norm - 2.0 * k["alpha"] * cross
        return softmax(-dist / (2.0 * k["t"] * math.sqrt(ncell)))

    w0 = weights(k0, z[:ROWS, :])
    cross = z[ROWS : 2 * ROWS, :] + k0["lift"] * lax.dot_general(
        w0, pp, NN, precision=lax.Precision.HIGHEST, preferred_element_type=F32
    )
    w1 = k1["lift"] * weights(k1, cross)
    w = jnp.concatenate([w0, w1], axis=0)
    wh = w.astype(BF)
    wl = (w - wh.astype(F32)).astype(BF)
    w2 = jnp.concatenate([wh, wl], axis=0)
    half = out.shape[1] // 2
    for h in range(2):
        pieces = [b[h] for b in blocks]

        def body(i, carry, h=h, pieces=pieces):
            where = pl.ds(pl.multiple_of(i * CHUNK, CHUNK), CHUNK)
            to = pl.ds(pl.multiple_of(i * CHUNK + h * half, CHUNK), CHUNK)
            x = jnp.concatenate([b[:, where] for b in pieces], axis=0)
            xh = x.astype(BF)
            xl = (x - xh.astype(F32)).astype(BF)
            m = lax.dot_general(w2, xh, NN, preferred_element_type=F32)
            m = m[: 2 * ROWS] + m[2 * ROWS :]
            m += lax.dot_general(wh, xl, NN, preferred_element_type=F32)
            out[:, to] = base[:, to] + ab[:, to] * m[:ROWS] + m[ROWS:]
            return carry

        lax.fori_loop(0, half // CHUNK, body, 0)


def final(ncell, z, base, ab, own, blocks):
    return pl.pallas_call(
        lambda *refs: final_kernel(ncell, *refs),
        out_shape=jax.ShapeDtypeStruct(own.shape, F32),
        cost_estimate=pl.CostEstimate(flops=10**9, bytes_accessed=6 * 10**6, transcendentals=0),
        name="final",
    )(z, base, ab, own, *blocks)


def total(x, size):
    for bits in (1, 2, 6, 8, 24):
        x = x + lax.ppermute(x, "cell", [(i, i ^ bits) for i in range(size)])
    return x


def per_device(prior, samples, noise, obs_cells, obs_values, seismic_mask):
    cells = prior.shape[1]
    half = cells // 2
    size = lax.axis_size("cell")
    ncell = cells * size
    up = [(i, (i + 1) % RINGS) for i in range(RINGS)]
    down = [(i, (i - 1) % RINGS) for i in range(RINGS)]
    rising = [prior[:, :half], prior[:, half:]]
    falling = list(rising)
    blocks = []
    for hop in range(3):
        for c in range(2):
            rising[c] = lax.ppermute(rising[c], "member", up)
            falling[c] = lax.ppermute(falling[c], "member", down)
        blocks += [*rising, *falling]
    far = [lax.ppermute(rising[0], "member", up), lax.ppermute(falling[1], "member", down)]
    u, base, ab = prep(obs_cells, obs_values, seismic_mask, samples, noise)
    early = gram(gram_kernel, (72, 56), samples, u, prior, *blocks)
    blocks += far
    z = gram(last_kernel, (80, 64), samples, u, prior, *blocks, early)
    z = total(z, size)
    return final(ncell, z, base, ab, prior, blocks)


def solution(mesh):
    in_specs = (
        P("member", "cell"),
        P("member", "cell"),
        P(None, "member", "cell"),
        P(None, "cell"),
        P(None, "cell"),
        P(None, "cell"),
    )
    out_specs = P("member", "cell")
    return jax.shard_map(
        per_device, mesh=mesh, in_specs=in_specs, out_specs=out_specs, check_vma=False
    )
```

```python
import math

import jax
import jax.numpy as jnp
from jax import lax
from jax.experimental import pallas as pl
from jax.experimental.pallas import tpu as pltpu
from jax.sharding import PartitionSpec as P

STEPS = 2
RINGS = 8
ROWS = 8
BF = jnp.bfloat16
F32 = jnp.float32
NT = (((1,), (1,)), ((), ()))
NN = (((1,), (0,)), ((), ()))


def constants(step):
    t = 0.6 - 0.1 * step
    alpha = 1.0 - 0.95 * t
    drift = -0.95 / alpha
    diffusion = 1.0 - 2.0 * drift * t
    return dict(
        t=t,
        alpha=alpha,
        gain=1.0 - 0.1 * drift - 0.1 * diffusion / t,
        pull=0.1 * diffusion * (1.0 - t),
        lift=0.1 * diffusion * alpha / t,
        kick=math.sqrt(0.1 * diffusion),
    )


def split3(x):
    a = x.astype(BF).astype(F32)
    r = x - a
    b = r.astype(BF).astype(F32)
    return a, b, r - b


def prep_kernel(cells, vals, mask, samples, noise, u_ref, base_ref, ab_ref, prec, targ):
    width = prec.shape[0]
    obs = cells.shape[1]
    rows = lax.broadcasted_iota(jnp.int32, (width, obs), 0)
    eye = lax.broadcasted_iota(jnp.int32, (width, width), 0) == lax.broadcasted_iota(
        jnp.int32, (width, width), 1
    )
    p_sum = jnp.zeros((width, width), F32)
    t_sum = jnp.zeros((width, width), F32)
    for s in range(cells.shape[0]):
        local = cells[s : s + 1, :] & (width * width - 1)
        high = jnp.where(rows == (local >> 7), 1.0, 0.0).astype(BF)
        low = rows == (local & 127)
        pieces = [jnp.ones((1, obs), F32), *split3(vals[s : s + 1, :])]
        sums = [
            lax.dot_general(
                high, jnp.where(low, piece, 0.0).astype(BF), NT, preferred_element_type=F32
            )
            for piece in pieces
        ]
        flags = mask[s : s + 1, :].astype(F32)
        flags = jnp.sum(jnp.where(eye, flags, 0.0), axis=1, keepdims=True)
        p_sum += flags * sums[0]
        t_sum += flags * (sums[1] + sums[2] + sums[3])
    prec[...] = p_sum
    targ[...] = t_sum
    k0, k1 = constants(0), constants(1)

    def body(h, carry):
        where = pl.ds(pl.multiple_of(h * width, width), width)
        p = prec[pl.ds(h, 1), :]
        t = targ[pl.ds(h, 1), :]
        u = (
            (k0["gain"] - k0["pull"] * p) * samples[:, where]
            + k0["pull"] * t
            + k0["kick"] * noise[0, :, where]
        )
        a1 = k1["gain"] - k1["pull"] * p
        u_ref[:, where] = u
        base_ref[:, where] = a1 * u + k1["pull"] * t + k1["kick"] * noise[1, :, where]
        ab_ref[:, where] = jnp.broadcast_to(k0["lift"] * a1, (ROWS, width))
        return carry

    lax.fori_loop(0, width, body, 0, unroll=4)


def prep(cells, vals, mask, samples, noise):
    shape = jax.ShapeDtypeStruct(samples.shape, F32)
    scratch = [pltpu.VMEM((128, 128), F32), pltpu.VMEM((128, 128), F32)]
    args = (cells, vals, mask, samples, noise)
    return call(prep_kernel, (shape, shape, shape), args, 10**9, scratch, name="prep")


CHUNK = 4096
LIMIT = pltpu.CompilerParams(vmem_limit_bytes=16 << 20)


def call(kernel, out_shape, args, flops, scratch=(), **kw):
    vmem = pl.BlockSpec(memory_space=pltpu.VMEM)
    return pl.pallas_call(
        kernel,
        out_shape=out_shape,
        in_specs=[vmem] * len(args),
        out_specs=jax.tree.map(lambda _: vmem, out_shape),
        scratch_shapes=scratch,
        compiler_params=LIMIT,
        cost_estimate=pl.CostEstimate(flops=flops, bytes_accessed=4 * 10**6, transcendentals=0),
        **kw,
    )(*args)


def split2(x):
    high = x.astype(BF).astype(F32)
    return jnp.concatenate([high, x - high], axis=0).astype(BF)


def column_chunks(blocks, body, acc):
    done = 0
    for pieces in zip(*blocks, strict=True):
        width = pieces[0].shape[1]
        for start in range(0, width, CHUNK):
            x = jnp.concatenate([p[:, start : start + CHUNK] for p in pieces], axis=0)
            acc = body(slice(done + start, done + start + CHUNK), x, acc)
        done += width
    return acc


def halves(full):
    half = full.shape[1] // 2
    return [full.at[:, :half], full.at[:, half:]]


def fold(z, m, n):
    z = z[:m] + z[m:]
    return z[:, :n] + z[:, n:]


def early_kernel(own, *refs):
    blocks, samples, u, z, stack = refs[:-4], *refs[-4:]
    blocks = [blocks[i : i + 2] for i in range(0, len(blocks), 2)]
    blocks = [halves(own), *blocks, halves(samples), halves(u)]

    def body(where, x, acc):
        y = split2(x)
        stack[:, where] = y
        return acc + lax.dot_general(y, y, NT, preferred_element_type=F32)

    rows = ROWS * len(blocks)
    acc = column_chunks(blocks, body, jnp.zeros((2 * rows, 2 * rows), F32))
    z[...] = fold(acc, rows, rows)[:, : rows - 2 * ROWS]


def early(samples, u, own, blocks):
    rows = ROWS * (3 + len(blocks) // 2)
    shapes = (
        jax.ShapeDtypeStruct((rows, rows - 2 * ROWS), F32),
        jax.ShapeDtypeStruct((2 * rows, own.shape[1]), BF),
    )
    return call(early_kernel, shapes, (own, *blocks, samples, u), 10**9, name="early")


def last_kernel(*refs):
    blocks, z1, stack, z, tail = refs[:-4], *refs[-4:]
    blocks = [blocks[i : i + 2] for i in range(0, len(blocks), 2)]
    new, old = ROWS * len(blocks), stack.shape[0] // 2

    def body(where, x, acc):
        y = split2(x)
        tail[:, where] = y
        a = jnp.concatenate([stack[:, where], y], axis=0)
        return acc + lax.dot_general(y, a, NT, preferred_element_type=F32)

    acc = column_chunks(blocks, body, jnp.zeros((2 * new, 2 * (old + new)), F32))
    acc = acc[:new] + acc[new:]
    left = acc[:, :old] + acc[:, old : 2 * old]
    right = acc[:, 2 * old : 2 * old + new] + acc[:, 2 * old + new :]
    m, n = z1.shape
    z[:m, :n] = z1[...]
    z[m:, :n] = left[:, :n]
    z[:m, n:] = left.T
    z[m:, n:] = right


def last(blocks, z1, stack):
    new = ROWS * (len(blocks) // 2)
    m, n = z1.shape
    shapes = (
        jax.ShapeDtypeStruct((m + new, n + new), F32),
        jax.ShapeDtypeStruct((2 * new, stack.shape[1]), BF),
    )
    return call(last_kernel, shapes, (*blocks, z1, stack), 10**9, name="last")


def softmax(x):
    e = jnp.exp(x - jnp.max(x, axis=1, keepdims=True))
    return e / jnp.sum(e, axis=1, keepdims=True)


def final_kernel(ncell, z_all, stack, tail, base, ab, out):
    z = z_all[0]
    for i in range(1, z_all.shape[0]):
        z = z + z_all[i]
    n = z.shape[1]
    old, new = stack.shape[0] // 2, tail.shape[0] // 2
    first = old - 2 * ROWS
    k0, k1 = constants(0), constants(1)
    pp = jnp.concatenate([z[:first], z[old:]], axis=0)
    eye = lax.broadcasted_iota(jnp.int32, (n, n), 0) == lax.broadcasted_iota(jnp.int32, (n, n), 1)
    norm = jnp.sum(jnp.where(eye, pp, 0.0), axis=0, keepdims=True)

    def weights(k, cross):
        dist = k["alpha"] * k["alpha"] * norm - 2.0 * k["alpha"] * cross
        return softmax(-dist / (2.0 * k["t"] * math.sqrt(ncell)))

    w0 = weights(k0, z[first : first + ROWS])
    cross = z[first + ROWS : old] + k0["lift"] * lax.dot_general(
        w0, pp, NN, precision=lax.Precision.HIGHEST, preferred_element_type=F32
    )
    w1 = k1["lift"] * weights(k1, cross)
    w = jnp.concatenate([w0, w1], axis=0)
    wh = w.astype(BF)
    w2 = jnp.concatenate([wh, (w - wh.astype(F32)).astype(BF)], axis=0)
    width = out.shape[1] // 2
    for start in range(0, out.shape[1], width):
        to = slice(start, start + width)
        high = jnp.concatenate([stack[:first, to], tail[:new, to]], axis=0)
        low = jnp.concatenate([stack[old : old + first, to], tail[new:, to]], axis=0)
        m = lax.dot_general(w2, high, NN, preferred_element_type=F32)
        m = m[: 2 * ROWS] + m[2 * ROWS :]
        m += lax.dot_general(wh, low, NN, preferred_element_type=F32)
        out[:, to] = base[:, to] + ab[:, to] * m[:ROWS] + m[ROWS:]


def final(ncell, z_all, stack, tail, base, ab):
    def final(*refs):
        return final_kernel(ncell, *refs)

    shape = jax.ShapeDtypeStruct(base.shape, F32)
    return call(final, shape, (z_all, stack, tail, base, ab), 10**9, name="final")


def per_device(prior, samples, noise, obs_cells, obs_values, seismic_mask):
    cells = prior.shape[1]
    half = cells // 2
    planes = lax.axis_size("x") * lax.axis_size("y")
    ncell = cells * planes * lax.axis_size("core")
    up = [(i, (i + 1) % RINGS) for i in range(RINGS)]
    down = [(i, (i - 1) % RINGS) for i in range(RINGS)]
    rising = [prior[:, :half], prior[:, half:]]
    falling = list(rising)
    blocks = []
    for hop in range(3):
        if hop == 2:
            rising[0], u = lax.optimization_barrier((rising[0], u))
        for c in range(2):
            rising[c] = lax.ppermute(rising[c], "member", up)
            falling[c] = lax.ppermute(falling[c], "member", down)
        blocks += [*rising, *falling]
        if hop == 0:
            rising[0], samples = lax.optimization_barrier((rising[0], samples))
            u, base, ab = prep(obs_cells, obs_values, seismic_mask, samples, noise)
    far = [lax.ppermute(rising[0], "member", up), lax.ppermute(falling[1], "member", down)]
    z1, stack = early(samples, u, prior, blocks[:8])
    z, tail = last((*blocks[8:], *far), z1, stack)
    z = z + lax.ppermute(z, "core", [(0, 1), (1, 0)])
    z = jnp.broadcast_to(z[None], (planes, *z.shape))
    z = lax.all_to_all(z, ("x", "y"), split_axis=0, concat_axis=0, tiled=True)
    return final(ncell, z, stack, tail, base, ab)


def solution(mesh):
    mesh = jax.sharding.Mesh(mesh.devices.reshape(RINGS, 4, 4, 2), ("member", "x", "y", "core"))
    cell = ("x", "y", "core")
    in_specs = (
        P("member", cell),
        P("member", cell),
        P(None, "member", cell),
        P(None, cell),
        P(None, cell),
        P(None, cell),
    )
    return jax.shard_map(
        per_device, mesh=mesh, in_specs=in_specs, out_specs=P("member", cell), check_vma=False
    )
```

```python
import math

import jax
import jax.numpy as jnp
from jax import lax
from jax.experimental import pallas as pl
from jax.experimental.pallas import tpu as pltpu
from jax.sharding import PartitionSpec as P

STEPS = 2
RINGS = 8
ROWS = 8
BF = jnp.bfloat16
F32 = jnp.float32
NT = (((1,), (1,)), ((), ()))
NN = (((1,), (0,)), ((), ()))


def constants(step):
    t = 0.6 - 0.1 * step
    alpha = 1.0 - 0.95 * t
    drift = -0.95 / alpha
    diffusion = 1.0 - 2.0 * drift * t
    return dict(
        t=t,
        alpha=alpha,
        gain=1.0 - 0.1 * drift - 0.1 * diffusion / t,
        pull=0.1 * diffusion * (1.0 - t),
        lift=0.1 * diffusion * alpha / t,
        kick=math.sqrt(0.1 * diffusion),
    )


def split3(x):
    a = x.astype(BF).astype(F32)
    r = x - a
    b = r.astype(BF).astype(F32)
    return a, b, r - b


def fields_kernel(cells, vals, mask, prec, targ):
    width = prec.shape[0]
    obs = cells.shape[1]
    rows = lax.broadcasted_iota(jnp.int32, (width, obs), 0)
    eye = lax.broadcasted_iota(jnp.int32, (width, width), 0) == lax.broadcasted_iota(
        jnp.int32, (width, width), 1
    )
    p_sum = jnp.zeros((width, width), F32)
    t_sum = jnp.zeros((width, width), F32)
    for s in range(cells.shape[0]):
        local = cells[s : s + 1, :] & (width * width - 1)
        high = jnp.where(rows == (local >> 7), 1.0, 0.0).astype(BF)
        low = rows == (local & 127)
        pieces = [jnp.ones((1, obs), F32), *split3(vals[s : s + 1, :])]
        sums = [
            lax.dot_general(
                high, jnp.where(low, piece, 0.0).astype(BF), NT, preferred_element_type=F32
            )
            for piece in pieces
        ]
        flags = mask[s : s + 1, :].astype(F32)
        flags = jnp.sum(jnp.where(eye, flags, 0.0), axis=1, keepdims=True)
        p_sum += flags * sums[0]
        t_sum += flags * (sums[1] + sums[2] + sums[3])
    prec[...] = p_sum
    targ[...] = t_sum


def fields(*args):
    shape = jax.ShapeDtypeStruct((128, 128), F32)
    return call(fields_kernel, (shape, shape), args, 10**9, name="fields")


def per_row(prec, targ, body):
    width = prec.shape[1]

    def step(h, carry):
        where = pl.ds(pl.multiple_of(h * width, width), width)
        body(where, prec[pl.ds(h, 1), :], targ[pl.ds(h, 1), :])
        return carry

    lax.fori_loop(0, prec.shape[0], step, 0, unroll=8)


def first_step(where, p, t, samples, noise):
    k = constants(0)
    return (
        (k["gain"] - k["pull"] * p) * samples[:, where]
        + k["pull"] * t
        + k["kick"] * noise[0, :, where]
    )


def base_kernel(samples, noise, prec, targ, base_ref, ab_ref):
    k0, k1 = constants(0), constants(1)

    def body(where, p, t):
        u = first_step(where, p, t, samples, noise)
        a1 = k1["gain"] - k1["pull"] * p
        base_ref[:, where] = a1 * u + k1["pull"] * t + k1["kick"] * noise[1, :, where]
        ab_ref[:, where] = jnp.broadcast_to(k0["lift"] * a1, u.shape)

    per_row(prec, targ, body)


def base_of(*args):
    shape = jax.ShapeDtypeStruct(args[0].shape, F32)
    return call(base_kernel, (shape, shape), args, 10**9, name="base")


CHUNK = 4096
LIMIT = pltpu.CompilerParams(vmem_limit_bytes=16 << 20)


def call(kernel, out_shape, args, flops, scratch=(), space=pltpu.VMEM, **kw):
    vmem = pl.BlockSpec(memory_space=pltpu.VMEM)
    return pl.pallas_call(
        kernel,
        out_shape=out_shape,
        in_specs=[pl.BlockSpec(memory_space=space)] * len(args),
        out_specs=jax.tree.map(lambda _: vmem, out_shape),
        scratch_shapes=scratch,
        compiler_params=LIMIT,
        cost_estimate=pl.CostEstimate(flops=flops, bytes_accessed=4 * 10**6, transcendentals=0),
        **kw,
    )(*args)


def split2(x):
    high = x.astype(BF).astype(F32)
    return jnp.concatenate([high, x - high], axis=0).astype(BF)


def column_chunks(blocks, body, acc):
    done = 0
    for pieces in zip(*blocks, strict=True):
        width = pieces[0].shape[1]
        for start in range(0, width, CHUNK):
            x = jnp.concatenate([p[:, start : start + CHUNK] for p in pieces], axis=0)
            acc = body(slice(done + start, done + start + CHUNK), x, acc)
        done += width
    return acc


def halves(full):
    half = full.shape[1] // 2
    return [full.at[:, :half], full.at[:, half:]]


def fold(z, m, n):
    z = z[:m] + z[m:]
    return z[:, :n] + z[:, n:]


def early_kernel(own, *refs):
    blocks, samples, noise, prec, targ, z, stack, u = refs[:-7], *refs[-7:]

    def first(where, p, t):
        u[:, where] = first_step(where, p, t, samples, noise)

    per_row(prec, targ, first)
    blocks = [blocks[i : i + 2] for i in range(0, len(blocks), 2)]
    blocks = [halves(own), *blocks, halves(samples), halves(u)]

    def body(where, x, acc):
        y = split2(x)
        stack[:, where] = y
        return acc + lax.dot_general(y, y, NT, preferred_element_type=F32)

    rows = ROWS * len(blocks)
    acc = column_chunks(blocks, body, jnp.zeros((2 * rows, 2 * rows), F32))
    z[...] = fold(acc, rows, rows)[:, : rows - 2 * ROWS]


def early(samples, noise, prec, targ, own, blocks):
    rows = ROWS * (3 + len(blocks) // 2)
    shapes = (
        jax.ShapeDtypeStruct((rows, rows - 2 * ROWS), F32),
        jax.ShapeDtypeStruct((2 * rows, own.shape[1]), BF),
    )
    args = (own, *blocks, samples, noise, prec, targ)
    return call(
        early_kernel, shapes, args, 10**9, [pltpu.VMEM(own.shape, F32)], name="early"
    )


def last_kernel(*refs):
    blocks, z1, stack, z, tail, full = refs[:-5], *refs[-5:]
    blocks = [blocks[i : i + 2] for i in range(0, len(blocks), 2)]
    new, old = ROWS * len(blocks), stack.shape[0] // 2

    def body(where, x, acc):
        y = split2(x)
        tail[:, where] = y
        return (
            acc[0] + lax.dot_general(y, stack[:, where], NT, preferred_element_type=F32),
            acc[1] + lax.dot_general(y, y, NT, preferred_element_type=F32),
        )

    acc = jnp.zeros((2 * new, 2 * old), F32), jnp.zeros((2 * new, 2 * new), F32)
    left, right = column_chunks(blocks, body, acc)
    left, right = fold(left, new, old), fold(right, new, new)
    m, n = z1.shape
    full[:m, :n] = z1[...]
    full[:m, n:] = left.T
    full[m:, :n] = left[:, :n]
    full[m:, n:] = right
    rows = z.shape[0]
    z[:, : n + new] = full[:rows, :]
    z[:, n + new :] = full[rows:, :]


def last(blocks, z1, stack):
    new = ROWS * (len(blocks) // 2)
    m, n = z1.shape
    shapes = (
        jax.ShapeDtypeStruct(((m + new) // 2, 2 * (n + new)), F32),
        jax.ShapeDtypeStruct((2 * new, stack.shape[1]), BF),
    )
    scratch = [pltpu.VMEM((m + new, n + new), F32)]
    return call(last_kernel, shapes, (*blocks, z1, stack), 10**9, scratch, name="last")


def softmax(x):
    e = jnp.exp(x - jnp.max(x, axis=1, keepdims=True))
    return e / jnp.sum(e, axis=1, keepdims=True)


def final_kernel(ncell, z_ref, stack, tail, base, ab, out):
    n = z_ref.shape[2] // 2
    old, new = stack.shape[0] // 2, tail.shape[0] // 2
    first = old - 2 * ROWS
    k0, k1 = constants(0), constants(1)
    z = z_ref[0]
    for i in range(1, z_ref.shape[0]):
        z = z + z_ref[i]
    z = jnp.concatenate([z[:, :n], z[:, n:]], axis=0)
    pp = jnp.concatenate([z[:first], z[old:]], axis=0)
    eye = lax.broadcasted_iota(jnp.int32, (n, n), 0) == lax.broadcasted_iota(jnp.int32, (n, n), 1)
    norm = jnp.sum(jnp.where(eye, pp, 0.0), axis=0, keepdims=True)

    def weights(k, cross):
        dist = k["alpha"] * k["alpha"] * norm - 2.0 * k["alpha"] * cross
        return softmax(-dist / (2.0 * k["t"] * math.sqrt(ncell)))

    w0 = weights(k0, z[first : first + ROWS])
    cross = z[first + ROWS : old] + k0["lift"] * lax.dot_general(
        w0, pp, NN, precision=lax.Precision.HIGHEST, preferred_element_type=F32
    )
    w1 = k1["lift"] * weights(k1, cross)
    w = jnp.concatenate([w0, w1], axis=0)
    wh = w.astype(BF).astype(F32)
    w = jnp.concatenate([wh, w - wh], axis=0)
    none = jnp.zeros((4 * ROWS, 2 * ROWS), F32)
    left = jnp.concatenate([w[:, :first], none, w[:, :first], none], axis=1).astype(BF)
    right = jnp.concatenate([w[:, first:], w[:, first:]], axis=1).astype(BF)
    width = out.shape[1] // 2
    for start in range(0, out.shape[1], width):
        to = slice(start, start + width)
        m = lax.dot_general(left, stack[:, to], NN, preferred_element_type=F32)
        m += lax.dot_general(right, tail[:, to], NN, preferred_element_type=F32)
        m = m[: 2 * ROWS] + m[2 * ROWS :]
        out[:, to] = base[:, to] + ab[:, to] * m[:ROWS] + m[ROWS:]


def final(ncell, z, stack, tail, base, ab):
    def final(*refs):
        return final_kernel(ncell, *refs)

    shape = jax.ShapeDtypeStruct(base.shape, F32)
    return call(final, shape, (z, stack, tail, base, ab), 10**9, name="final")


def total(x):
    x = x + lax.ppermute(x, "core", [(0, 1), (1, 0)])
    x = jnp.broadcast_to(x[None], (lax.axis_size("x") * lax.axis_size("y"), *x.shape))
    return lax.all_to_all(x, ("x", "y"), split_axis=0, concat_axis=0, tiled=True)


def per_device(prior, samples, noise, obs_cells, obs_values, seismic_mask):
    cells = prior.shape[1]
    half = cells // 2
    ncell = cells * lax.axis_size("x") * lax.axis_size("y") * lax.axis_size("core")
    up = [(i, (i + 1) % RINGS) for i in range(RINGS)]
    down = [(i, (i - 1) % RINGS) for i in range(RINGS)]
    rising = [prior[:, :half], prior[:, half:]]
    falling = list(rising)
    blocks = []
    prec, targ = fields(obs_cells, obs_values, seismic_mask)
    base, ab = base_of(samples, noise, prec, targ)
    for hop in range(3):
        if hop == 1:
            rising[0], prec, targ = lax.optimization_barrier((rising[0], prec, targ))
        if hop == 2:
            rising[0], base, ab = lax.optimization_barrier((rising[0], base, ab))
        for c in range(2):
            rising[c] = lax.ppermute(rising[c], "member", up)
            falling[c] = lax.ppermute(falling[c], "member", down)
        blocks += [*rising, *falling]
    z1, stack = early(samples, noise, prec, targ, prior, blocks)
    far = [lax.ppermute(rising[0], "member", up), lax.ppermute(falling[1], "member", down)]
    z, tail = last(far, z1, stack)
    z = total(z)
    return final(ncell, z, stack, tail, base, ab)


def solution(mesh):
    mesh = jax.sharding.Mesh(mesh.devices.reshape(RINGS, 4, 4, 2), ("member", "x", "y", "core"))
    cell = ("x", "y", "core")
    in_specs = (
        P("member", cell),
        P("member", cell),
        P(None, "member", cell),
        P(None, cell),
        P(None, cell),
        P(None, cell),
    )
    return jax.shard_map(
        per_device, mesh=mesh, in_specs=in_specs, out_specs=P("member", cell), check_vma=False
    )
```

```python
import math

import jax
import jax.numpy as jnp
from jax import lax
from jax.experimental import pallas as pl
from jax.experimental.pallas import tpu as pltpu
from jax.sharding import PartitionSpec as P

STEPS = 2
RINGS = 8
ROWS = 8
BF = jnp.bfloat16
F32 = jnp.float32
NT = (((1,), (1,)), ((), ()))
NN = (((1,), (0,)), ((), ()))


def constants(step):
    t = 0.6 - 0.1 * step
    alpha = 1.0 - 0.95 * t
    drift = -0.95 / alpha
    diffusion = 1.0 - 2.0 * drift * t
    return dict(
        t=t,
        alpha=alpha,
        gain=1.0 - 0.1 * drift - 0.1 * diffusion / t,
        pull=0.1 * diffusion * (1.0 - t),
        lift=0.1 * diffusion * alpha / t,
        kick=math.sqrt(0.1 * diffusion),
    )


def split3(x):
    a = x.astype(BF).astype(F32)
    r = x - a
    b = r.astype(BF).astype(F32)
    return a, b, r - b


def fields_kernel(cells, vals, mask, prec, targ):
    width = prec.shape[0]
    obs = cells.shape[1]
    rows = lax.broadcasted_iota(jnp.int32, (width, obs), 0)
    eye = lax.broadcasted_iota(jnp.int32, (width, width), 0) == lax.broadcasted_iota(
        jnp.int32, (width, width), 1
    )
    p_sum = jnp.zeros((width, width), F32)
    t_sum = jnp.zeros((width, width), F32)
    for s in range(cells.shape[0]):
        local = cells[s : s + 1, :] & (width * width - 1)
        high = jnp.where(rows == (local >> 7), 1.0, 0.0).astype(BF)
        low = rows == (local & 127)
        pieces = [jnp.ones((1, obs), F32), *split3(vals[s : s + 1, :])]
        sums = [
            lax.dot_general(
                high, jnp.where(low, piece, 0.0).astype(BF), NT, preferred_element_type=F32
            )
            for piece in pieces
        ]
        flags = mask[s : s + 1, :].astype(F32)
        flags = jnp.sum(jnp.where(eye, flags, 0.0), axis=1, keepdims=True)
        p_sum += flags * sums[0]
        t_sum += flags * (sums[1] + sums[2] + sums[3])
    prec[...] = p_sum
    targ[...] = t_sum


def fields(*args):
    shape = jax.ShapeDtypeStruct((128, 128), F32)
    return call(fields_kernel, (shape, shape), args, 10**9, name="fields")


def per_row(prec, targ, body):
    width = prec.shape[1]

    def step(h, carry):
        where = pl.ds(pl.multiple_of(h * width, width), width)
        body(where, prec[pl.ds(h, 1), :], targ[pl.ds(h, 1), :])
        return carry

    lax.fori_loop(0, prec.shape[0], step, 0, unroll=8)


CHUNK = 4096
LIMIT = pltpu.CompilerParams(vmem_limit_bytes=16 << 20)


def call(kernel, out_shape, args, flops, scratch=(), space=pltpu.VMEM, out_space=pltpu.VMEM, **kw):
    out_spec = pl.BlockSpec(memory_space=out_space)
    return pl.pallas_call(
        kernel,
        out_shape=out_shape,
        in_specs=[pl.BlockSpec(memory_space=space)] * len(args),
        out_specs=jax.tree.map(lambda _: out_spec, out_shape),
        scratch_shapes=scratch,
        compiler_params=LIMIT,
        cost_estimate=pl.CostEstimate(flops=flops, bytes_accessed=4 * 10**6, transcendentals=0),
        **kw,
    )(*args)


def split2(x):
    high = x.astype(BF).astype(F32)
    return jnp.concatenate([high, x - high], axis=0).astype(BF)


def column_chunks(blocks, body, acc):
    done = 0
    for pieces in zip(*blocks, strict=True):
        width = pieces[0].shape[1]
        for start in range(0, width, CHUNK):
            x = jnp.concatenate([p[:, start : start + CHUNK] for p in pieces], axis=0)
            acc = body(slice(done + start, done + start + CHUNK), x, acc)
        done += width
    return acc


def halves(full):
    half = full.shape[1] // 2
    return [full.at[:, :half], full.at[:, half:]]


def fold(z, m, n):
    z = z[:m] + z[m:]
    return z[:, :n] + z[:, n:]


def early_kernel(own, *refs):
    blocks, samples, noise, prec, targ, z, stack, base, ab, u = refs[:-9], *refs[-9:]
    k0, k1 = constants(0), constants(1)

    def local(where, p, t):
        a1 = k1["gain"] - k1["pull"] * p
        x = (k0["gain"] - k0["pull"] * p) * samples[:, where]
        x = x + k0["pull"] * t + k0["kick"] * noise[0, :, where]
        u[:, where] = x
        base[:, where] = a1 * x + k1["pull"] * t + k1["kick"] * noise[1, :, where]
        ab[:, where] = jnp.broadcast_to(k0["lift"] * a1, x.shape)

    per_row(prec, targ, local)
    blocks = [blocks[i : i + 2] for i in range(0, len(blocks), 2)]
    blocks = [halves(own), *blocks, halves(samples), halves(u)]

    def body(where, x, acc):
        y = split2(x)
        stack[: y.shape[0], where] = y
        return acc + lax.dot_general(y, y, NT, preferred_element_type=F32)

    rows = ROWS * len(blocks)
    acc = column_chunks(blocks, body, jnp.zeros((2 * rows, 2 * rows), F32))
    acc = fold(acc, rows, rows)
    near, q = rows - 2 * ROWS, z.shape[0]
    z[...] = jnp.zeros(z.shape, F32)
    z[:, :near] = acc[:q, :near]
    z[: near - q, 2 * q : q + near] = acc[q:near, q:near]
    z[: 2 * ROWS, 3 * q :] = acc[near:, :q]
    z[2 * ROWS :, 3 * q : 2 * q + near] = acc[near:, q:near]


def early(samples, noise, prec, targ, own, blocks):
    rows = ROWS * (3 + len(blocks) // 2)
    shapes = (
        jax.ShapeDtypeStruct((ROWS * RINGS // 2, 2 * ROWS * RINGS), F32),
        jax.ShapeDtypeStruct((2 * (rows + ROWS), own.shape[1]), BF),
        jax.ShapeDtypeStruct(own.shape, F32),
        jax.ShapeDtypeStruct(own.shape, F32),
    )
    args = (own, *blocks, samples, noise, prec, targ)
    return call(
        early_kernel, shapes, args, 10**9, [pltpu.VMEM(own.shape, F32)], name="early"
    )


def last_kernel(*refs):
    far, z1, _, z, stack = refs[:-4], *refs[-4:]
    new, old = ROWS, stack.shape[0] // 2 - ROWS

    def body(where, x, acc):
        y = split2(x)
        stack[2 * old :, where] = y
        return acc + lax.dot_general(y, stack[:, where], NT, preferred_element_type=F32)

    acc = column_chunks([far], body, jnp.zeros((2 * new, 2 * (old + new)), F32))
    left, right = fold(acc[:, : 2 * old], new, old), fold(acc[:, 2 * old :], new, new)
    near, q = old - 2 * ROWS, z.shape[0]
    column = left.T
    z[...] = z1[...]
    z[:, near : 2 * q] = column[:q]
    z[: near - q, q + near : 3 * q] = column[q:near]
    z[near - q :, 2 * q : q + near] = left[:, q:near]
    z[near - q :, q + near : 3 * q] = right
    z[2 * ROWS :, 2 * q + near :] = column[near:]


def last(far, z1, stack):
    shapes = (jax.ShapeDtypeStruct(z1.shape, F32), jax.ShapeDtypeStruct(stack.shape, BF))
    args = (*far, z1, stack)
    places = {len(args) - 1: 1}
    return call(last_kernel, shapes, args, 10**9, input_output_aliases=places, name="last")


def exponentials(x):
    e = jnp.exp(x - jnp.max(x, axis=1, keepdims=True))
    return e, 1.0 / jnp.sum(e, axis=1, keepdims=True)


def final_kernel(ncell, z_ref, stack, base, ab, out, buffer, sems):
    first = stack.shape[0] // 2 - 3 * ROWS
    k0, k1 = constants(0), constants(1)
    z = z_ref[0]
    for i in range(1, z_ref.shape[0]):
        z = z + z_ref[i]
    q = z.shape[0]
    corner, side, other, rest = [z[:, i * q : (i + 1) * q] for i in range(4)]
    eye = lax.broadcasted_iota(jnp.int32, (q, q), 0) == lax.broadcasted_iota(jnp.int32, (q, q), 1)
    norm = [jnp.sum(jnp.where(eye, x, 0.0), axis=0, keepdims=True) for x in (corner, other)]
    norm = jnp.concatenate(norm, axis=1)
    members = jnp.concatenate([z[:, : 2 * q], jnp.concatenate([side.T, other], axis=1)], axis=0)
    cross = jnp.concatenate([rest[: 2 * ROWS], rest[2 * ROWS :]], axis=1)

    def terms(k, cross):
        dist = k["alpha"] * k["alpha"] * norm - 2.0 * k["alpha"] * cross
        return exponentials(dist * (-1.0 / (2.0 * k["t"] * math.sqrt(ncell))))

    def dot(x, y):
        return lax.dot_general(
            x, y, NN, precision=lax.Precision.HIGHEST, preferred_element_type=F32
        )

    e0, scale0 = terms(k0, cross[:ROWS])
    lift = dot(e0, members)
    e1, scale1 = terms(k1, cross[ROWS:] + k0["lift"] * (scale0 * lift))
    scale1 = k1["lift"] * scale1
    w = jnp.concatenate([e0, e1], axis=0)
    wh = w.astype(BF).astype(F32)
    w = jnp.concatenate([wh, w - wh], axis=0)
    none = jnp.zeros((4 * ROWS, 2 * ROWS), F32)
    near = jnp.concatenate([w[:, :first], none], axis=1)
    w = jnp.concatenate([near, near, w[:, first:], w[:, first:]], axis=1).astype(BF)
    pieces = sems.shape[0]
    width = out.shape[1] // pieces
    copies = []
    for i in range(pieces):
        to = slice(i * width, (i + 1) * width)
        m = lax.dot_general(w, stack[:, to], NN, preferred_element_type=F32)
        m = m[: 2 * ROWS] + m[2 * ROWS :]
        buffer[:, to] = base[:, to] + ab[:, to] * (scale0 * m[:ROWS]) + scale1 * m[ROWS:]
        copies.append(pltpu.make_async_copy(buffer.at[:, to], out.at[:, to], sems.at[i]))
        copies[-1].start()
    for copy in copies:
        copy.wait()


def final(ncell, z, stack, base, ab):
    def final(*refs):
        return final_kernel(ncell, *refs)

    shape = jax.ShapeDtypeStruct(base.shape, F32)
    scratch = [pltpu.VMEM(base.shape, F32), pltpu.SemaphoreType.DMA((4,))]
    args = (z, stack, base, ab)
    return call(final, shape, args, 10**9, scratch, out_space=pltpu.HBM, name="final")


def total(x):
    x = x + lax.ppermute(x, "core", [(0, 1), (1, 0)])
    x = jnp.broadcast_to(x[None], (lax.axis_size("x") * lax.axis_size("y"), *x.shape))
    return lax.all_to_all(x, ("x", "y"), split_axis=0, concat_axis=0, tiled=True)


def per_device(prior, samples, noise, obs_cells, obs_values, seismic_mask):
    cells = prior.shape[1]
    half = cells // 2
    ncell = cells * lax.axis_size("x") * lax.axis_size("y") * lax.axis_size("core")
    up = [(i, (i + 1) % RINGS) for i in range(RINGS)]
    down = [(i, (i - 1) % RINGS) for i in range(RINGS)]
    rising = [prior[:, :half], prior[:, half:]]
    falling = list(rising)
    blocks = []
    prec, targ = fields(obs_cells, obs_values, seismic_mask)
    for hop in range(3):
        if hop == 1:
            rising[0], prec, targ = lax.optimization_barrier((rising[0], prec, targ))
        for c in range(2):
            rising[c] = lax.ppermute(rising[c], "member", up)
            falling[c] = lax.ppermute(falling[c], "member", down)
        blocks += [*rising, *falling]
    z1, stack, base, ab = early(samples, noise, prec, targ, prior, blocks)
    far = [lax.ppermute(rising[0], "member", up), lax.ppermute(falling[1], "member", down)]
    z, stack = last(far, z1, stack)
    z = total(z)
    return final(ncell, z, stack, base, ab)


def solution(mesh):
    mesh = jax.sharding.Mesh(mesh.devices.reshape(RINGS, 4, 4, 2), ("member", "x", "y", "core"))
    cell = ("x", "y", "core")
    in_specs = (
        P("member", cell),
        P("member", cell),
        P(None, "member", cell),
        P(None, cell),
        P(None, cell),
        P(None, cell),
    )
    return jax.shard_map(
        per_device, mesh=mesh, in_specs=in_specs, out_specs=P("member", cell), check_vma=False
    )
```

```python
import math

import jax
import jax.numpy as jnp
from jax import lax
from jax.experimental import pallas as pl
from jax.experimental.pallas import tpu as pltpu
from jax.sharding import PartitionSpec as P

STEPS = 2
RINGS = 8
ROWS = 8
BF = jnp.bfloat16
F32 = jnp.float32
NT = (((1,), (1,)), ((), ()))
NN = (((1,), (0,)), ((), ()))


def constants(step):
    t = 0.6 - 0.1 * step
    alpha = 1.0 - 0.95 * t
    drift = -0.95 / alpha
    diffusion = 1.0 - 2.0 * drift * t
    return dict(
        t=t,
        alpha=alpha,
        gain=1.0 - 0.1 * drift - 0.1 * diffusion / t,
        pull=0.1 * diffusion * (1.0 - t),
        lift=0.1 * diffusion * alpha / t,
        kick=math.sqrt(0.1 * diffusion),
    )


def split3(x):
    a = x.astype(BF).astype(F32)
    r = x - a
    b = r.astype(BF).astype(F32)
    return a, b, r - b


def fields_kernel(cells, vals, mask, prec, targ):
    width = prec.shape[0]
    obs = cells.shape[1]
    rows = lax.broadcasted_iota(jnp.int32, (width, obs), 0)
    eye = lax.broadcasted_iota(jnp.int32, (width, width), 0) == lax.broadcasted_iota(
        jnp.int32, (width, width), 1
    )
    p_sum = jnp.zeros((width, width), F32)
    t_sum = jnp.zeros((width, width), F32)
    for s in range(cells.shape[0]):
        local = cells[s : s + 1, :] & (width * width - 1)
        high = jnp.where(rows == (local >> 7), 1.0, 0.0).astype(BF)
        low = rows == (local & 127)
        pieces = [jnp.ones((1, obs), F32), *split3(vals[s : s + 1, :])]
        sums = [
            lax.dot_general(
                high, jnp.where(low, piece, 0.0).astype(BF), NT, preferred_element_type=F32
            )
            for piece in pieces
        ]
        flags = mask[s : s + 1, :].astype(F32)
        flags = jnp.sum(jnp.where(eye, flags, 0.0), axis=1, keepdims=True)
        p_sum += flags * sums[0]
        t_sum += flags * (sums[1] + sums[2] + sums[3])
    prec[...] = p_sum
    targ[...] = t_sum


def fields(*args):
    shape = jax.ShapeDtypeStruct((128, 128), F32)
    return call(fields_kernel, (shape, shape), args, 10**9, name="fields")


def per_row(prec, targ, body):
    width = prec.shape[1]

    def step(h, carry):
        where = pl.ds(pl.multiple_of(h * width, width), width)
        body(where, prec[pl.ds(h, 1), :], targ[pl.ds(h, 1), :])
        return carry

    lax.fori_loop(0, prec.shape[0], step, 0, unroll=8)


CHUNK = 4096
LIMIT = pltpu.CompilerParams(vmem_limit_bytes=16 << 20)


def call(kernel, out_shape, args, flops, scratch=(), space=pltpu.VMEM, out_space=pltpu.VMEM, **kw):
    out_spec = pl.BlockSpec(memory_space=out_space)
    return pl.pallas_call(
        kernel,
        out_shape=out_shape,
        in_specs=[pl.BlockSpec(memory_space=space)] * len(args),
        out_specs=jax.tree.map(lambda _: out_spec, out_shape),
        scratch_shapes=scratch,
        compiler_params=LIMIT,
        cost_estimate=pl.CostEstimate(flops=flops, bytes_accessed=4 * 10**6, transcendentals=0),
        **kw,
    )(*args)


def split2(x):
    high = x.astype(BF).astype(F32)
    return jnp.concatenate([high, x - high], axis=0).astype(BF)


def column_chunks(blocks, body, acc):
    done = 0
    for pieces in zip(*blocks, strict=True):
        width = pieces[0].shape[1]
        for start in range(0, width, CHUNK):
            x = jnp.concatenate([p[:, start : start + CHUNK] for p in pieces], axis=0)
            acc = body(slice(done + start, done + start + CHUNK), x, acc)
        done += width
    return acc


def halves(full):
    half = full.shape[1] // 2
    return [full.at[:, :half], full.at[:, half:]]


def fold(z, m, n):
    z = z[:m] + z[m:]
    return z[:, :n] + z[:, n:]


def early_kernel(own, *refs):
    blocks, samples, noise, prec, targ, z, stack, base, ab, u = refs[:-9], *refs[-9:]
    k0, k1 = constants(0), constants(1)

    def local(where, p, t):
        a1 = k1["gain"] - k1["pull"] * p
        x = (k0["gain"] - k0["pull"] * p) * samples[:, where]
        x = x + k0["pull"] * t + k0["kick"] * noise[0, :, where]
        u[:, where] = x
        base[:, where] = a1 * x + k1["pull"] * t + k1["kick"] * noise[1, :, where]
        ab[:, where] = jnp.broadcast_to(k0["lift"] * a1, x.shape)

    per_row(prec, targ, local)
    blocks = [blocks[i : i + 2] for i in range(0, len(blocks), 2)]
    blocks = [halves(own), *blocks, halves(samples), halves(u)]

    def body(where, x, acc):
        y = split2(x)
        stack[: y.shape[0], where] = y
        return acc + lax.dot_general(y, y, NT, preferred_element_type=F32)

    rows = ROWS * len(blocks)
    acc = column_chunks(blocks, body, jnp.zeros((2 * rows, 2 * rows), F32))
    acc = fold(acc, rows, rows)
    near, q = rows - 2 * ROWS, z.shape[0]
    z[...] = jnp.zeros(z.shape, F32)
    z[:, :near] = acc[:q, :near]
    z[: near - q, 2 * q : q + near] = acc[q:near, q:near]
    z[: 2 * ROWS, 3 * q :] = acc[near:, :q]
    z[2 * ROWS :, 3 * q : 2 * q + near] = acc[near:, q:near]


def early(samples, noise, prec, targ, own, blocks):
    rows = ROWS * (3 + len(blocks) // 2)
    shapes = (
        jax.ShapeDtypeStruct((ROWS * RINGS // 2, 2 * ROWS * RINGS), F32),
        jax.ShapeDtypeStruct((2 * (rows + ROWS), own.shape[1]), BF),
        jax.ShapeDtypeStruct(own.shape, F32),
        jax.ShapeDtypeStruct(own.shape, F32),
    )
    args = (own, *blocks, samples, noise, prec, targ)
    return call(
        early_kernel, shapes, args, 10**9, [pltpu.VMEM(own.shape, F32)], name="early"
    )


def last_kernel(*refs):
    far, z1, _, z, stack = refs[:-4], *refs[-4:]
    new, old = ROWS, stack.shape[0] // 2 - ROWS

    def body(where, x, acc):
        y = split2(x)
        stack[2 * old :, where] = y
        return acc + lax.dot_general(y, stack[:, where], NT, preferred_element_type=F32)

    acc = column_chunks([far], body, jnp.zeros((2 * new, 2 * (old + new)), F32))
    left, right = fold(acc[:, : 2 * old], new, old), fold(acc[:, 2 * old :], new, new)
    near, q = old - 2 * ROWS, z.shape[0]
    column = left.T
    z[...] = z1[...]
    z[:, near : 2 * q] = column[:q]
    z[: near - q, q + near : 3 * q] = column[q:near]
    z[near - q :, 2 * q : q + near] = left[:, q:near]
    z[near - q :, q + near : 3 * q] = right
    z[2 * ROWS :, 2 * q + near :] = column[near:]


def last(far, z1, stack):
    shapes = (jax.ShapeDtypeStruct(z1.shape, F32), jax.ShapeDtypeStruct(stack.shape, BF))
    args = (*far, z1, stack)
    places = {len(args) - 1: 1}
    return call(last_kernel, shapes, args, 10**9, input_output_aliases=places, name="last")


def exponentials(x):
    e = jnp.exp(x - jnp.max(x, axis=1, keepdims=True))
    return e, 1.0 / jnp.sum(e, axis=1, keepdims=True)


def final_kernel(ncell, z_ref, stack, base, ab, out, buffer, sems):
    first = stack.shape[0] // 2 - 3 * ROWS
    k0, k1 = constants(0), constants(1)
    z = z_ref[0]
    for i in range(1, z_ref.shape[0]):
        z = z + z_ref[i]
    q = z.shape[0]
    corner, side, other, rest = [z[:, i * q : (i + 1) * q] for i in range(4)]
    eye = lax.broadcasted_iota(jnp.int32, (q, q), 0) == lax.broadcasted_iota(jnp.int32, (q, q), 1)
    norm = [jnp.sum(jnp.where(eye, x, 0.0), axis=0, keepdims=True) for x in (corner, other)]
    norm = jnp.concatenate(norm, axis=1)
    members = jnp.concatenate([z[:, : 2 * q], jnp.concatenate([side.T, other], axis=1)], axis=0)
    cross = jnp.concatenate([rest[: 2 * ROWS], rest[2 * ROWS :]], axis=1)

    def terms(k, cross):
        dist = k["alpha"] * k["alpha"] * norm - 2.0 * k["alpha"] * cross
        return exponentials(dist * (-1.0 / (2.0 * k["t"] * math.sqrt(ncell))))

    def dot(x, y):
        return lax.dot_general(
            x, y, NN, precision=lax.Precision.HIGHEST, preferred_element_type=F32
        )

    e0, scale0 = terms(k0, cross[:ROWS])
    e1, scale1 = terms(k1, cross[ROWS:] + k0["lift"] * dot(e0 * scale0, members))
    scale1 = k1["lift"] * scale1
    w = jnp.concatenate([e0, e1], axis=0)
    wh = w.astype(BF).astype(F32)
    w = jnp.concatenate([wh, w - wh], axis=0)
    none = jnp.zeros((4 * ROWS, 2 * ROWS), F32)
    near = jnp.concatenate([w[:, :first], none], axis=1)
    w = jnp.concatenate([near, near, w[:, first:], w[:, first:]], axis=1).astype(BF)
    pieces = sems.shape[0]
    width = out.shape[1] // pieces
    copies = []
    for i in range(pieces):
        to = slice(i * width, (i + 1) * width)
        m = lax.dot_general(w, stack[:, to], NN, preferred_element_type=F32)
        m = m[: 2 * ROWS] + m[2 * ROWS :]
        buffer[:, to] = base[:, to] + ab[:, to] * (scale0 * m[:ROWS]) + scale1 * m[ROWS:]
        copies.append(pltpu.make_async_copy(buffer.at[:, to], out.at[:, to], sems.at[i]))
        copies[-1].start()
    for copy in copies:
        copy.wait()


def final(ncell, z, stack, base, ab):
    def final(*refs):
        return final_kernel(ncell, *refs)

    shape = jax.ShapeDtypeStruct(base.shape, F32)
    scratch = [pltpu.VMEM(base.shape, F32), pltpu.SemaphoreType.DMA((4,))]
    args = (z, stack, base, ab)
    return call(final, shape, args, 10**9, scratch, out_space=pltpu.HBM, name="final")


def total(x):
    x = x + lax.ppermute(x, "core", [(0, 1), (1, 0)])
    x = jnp.broadcast_to(x[None], (lax.axis_size("x") * lax.axis_size("y"), *x.shape))
    return lax.all_to_all(x, ("x", "y"), split_axis=0, concat_axis=0, tiled=True)


def per_device(prior, samples, noise, obs_cells, obs_values, seismic_mask):
    cells = prior.shape[1]
    half = cells // 2
    ncell = cells * lax.axis_size("x") * lax.axis_size("y") * lax.axis_size("core")
    up = [(i, (i + 1) % RINGS) for i in range(RINGS)]
    down = [(i, (i - 1) % RINGS) for i in range(RINGS)]
    rising = [prior[:, :half], prior[:, half:]]
    falling = list(rising)
    blocks = []
    prec, targ = fields(obs_cells, obs_values, seismic_mask)
    for hop in range(3):
        if hop > 0:
            rising[0], prec, targ = lax.optimization_barrier((rising[0], prec, targ))
        for c in range(2):
            rising[c] = lax.ppermute(rising[c], "member", up)
            falling[c] = lax.ppermute(falling[c], "member", down)
        blocks += [*rising, *falling]
    rising[0], prec, targ = lax.optimization_barrier((rising[0], prec, targ))
    z1, stack, base, ab = early(samples, noise, prec, targ, prior, blocks)
    far = [lax.ppermute(rising[0], "member", up), lax.ppermute(falling[1], "member", down)]
    z, stack = last(far, z1, stack)
    z = total(z)
    return final(ncell, z, stack, base, ab)


def solution(mesh):
    mesh = jax.sharding.Mesh(mesh.devices.reshape(RINGS, 4, 4, 2), ("member", "x", "y", "core"))
    cell = ("x", "y", "core")
    in_specs = (
        P("member", cell),
        P("member", cell),
        P(None, "member", cell),
        P(None, cell),
        P(None, cell),
        P(None, cell),
    )
    return jax.shard_map(
        per_device, mesh=mesh, in_specs=in_specs, out_specs=P("member", cell), check_vma=False
    )
```

```python
import math

import jax
import jax.numpy as jnp
from jax import lax
from jax.experimental import pallas as pl
from jax.experimental.pallas import tpu as pltpu
from jax.sharding import PartitionSpec as P

STEPS = 2
RINGS = 8
ROWS = 8
BF = jnp.bfloat16
F32 = jnp.float32
NT = (((1,), (1,)), ((), ()))
NN = (((1,), (0,)), ((), ()))


def constants(step):
    t = 0.6 - 0.1 * step
    alpha = 1.0 - 0.95 * t
    drift = -0.95 / alpha
    diffusion = 1.0 - 2.0 * drift * t
    return dict(
        t=t,
        alpha=alpha,
        gain=1.0 - 0.1 * drift - 0.1 * diffusion / t,
        pull=0.1 * diffusion * (1.0 - t),
        lift=0.1 * diffusion * alpha / t,
        kick=math.sqrt(0.1 * diffusion),
    )


def split3(x):
    a = x.astype(BF).astype(F32)
    r = x - a
    b = r.astype(BF).astype(F32)
    return a, b, r - b


def fields_kernel(cells, vals, mask, prec, targ):
    width = prec.shape[0]
    obs = cells.shape[1]
    rows = lax.broadcasted_iota(jnp.int32, (width, obs), 0)
    eye = lax.broadcasted_iota(jnp.int32, (width, width), 0) == lax.broadcasted_iota(
        jnp.int32, (width, width), 1
    )
    p_sum = jnp.zeros((width, width), F32)
    t_sum = jnp.zeros((width, width), F32)
    for s in range(cells.shape[0]):
        local = cells[s : s + 1, :] & (width * width - 1)
        high = jnp.where(rows == (local >> 7), 1.0, 0.0).astype(BF)
        low = rows == (local & 127)
        pieces = [jnp.ones((1, obs), F32), *split3(vals[s : s + 1, :])]
        sums = [
            lax.dot_general(
                high, jnp.where(low, piece, 0.0).astype(BF), NT, preferred_element_type=F32
            )
            for piece in pieces
        ]
        flags = mask[s : s + 1, :].astype(F32)
        flags = jnp.sum(jnp.where(eye, flags, 0.0), axis=1, keepdims=True)
        p_sum += flags * sums[0]
        t_sum += flags * (sums[1] + sums[2] + sums[3])
    prec[...] = p_sum
    targ[...] = t_sum


def fields(*args):
    shape = jax.ShapeDtypeStruct((128, 128), F32)
    return call(fields_kernel, (shape, shape), args, 10**9, name="fields")


def per_row(prec, targ, body):
    width = prec.shape[1]

    def step(h, carry):
        where = pl.ds(pl.multiple_of(h * width, width), width)
        body(where, prec[pl.ds(h, 1), :], targ[pl.ds(h, 1), :])
        return carry

    lax.fori_loop(0, prec.shape[0], step, 0, unroll=8)


def local_kernel(samples, noise, prec, targ, u, base, ab):
    k0, k1 = constants(0), constants(1)

    def local(where, p, t):
        a1 = k1["gain"] - k1["pull"] * p
        x = (k0["gain"] - k0["pull"] * p) * samples[:, where]
        x = x + k0["pull"] * t + k0["kick"] * noise[0, :, where]
        u[:, where] = x
        base[:, where] = a1 * x + k1["pull"] * t + k1["kick"] * noise[1, :, where]
        ab[:, where] = jnp.broadcast_to(k0["lift"] * a1, x.shape)

    per_row(prec, targ, local)


def local_terms(*args):
    shape = jax.ShapeDtypeStruct(args[0].shape, F32)
    return call(local_kernel, (shape, shape, shape), args, 10**9, name="local")


CHUNK = 4096
LIMIT = pltpu.CompilerParams(vmem_limit_bytes=16 << 20)


def call(kernel, out_shape, args, flops, scratch=(), space=pltpu.VMEM, out_space=pltpu.VMEM, **kw):
    out_spec = pl.BlockSpec(memory_space=out_space)
    return pl.pallas_call(
        kernel,
        out_shape=out_shape,
        in_specs=[pl.BlockSpec(memory_space=space)] * len(args),
        out_specs=jax.tree.map(lambda _: out_spec, out_shape),
        scratch_shapes=scratch,
        compiler_params=LIMIT,
        cost_estimate=pl.CostEstimate(flops=flops, bytes_accessed=4 * 10**6, transcendentals=0),
        **kw,
    )(*args)


def split2(x):
    high = x.astype(BF).astype(F32)
    return jnp.concatenate([high, x - high], axis=0).astype(BF)


def column_chunks(blocks, body, acc):
    done = 0
    for pieces in zip(*blocks, strict=True):
        width = pieces[0].shape[1]
        for start in range(0, width, CHUNK):
            x = jnp.concatenate([p[:, start : start + CHUNK] for p in pieces], axis=0)
            acc = body(slice(done + start, done + start + CHUNK), x, acc)
        done += width
    return acc


def halves(full):
    half = full.shape[1] // 2
    return [full.at[:, :half], full.at[:, half:]]


def fold(z, m, n):
    z = z[:m] + z[m:]
    return z[:, :n] + z[:, n:]


def early_kernel(own, *refs):
    blocks, samples, u, z, stack = refs[:-4], *refs[-4:]
    blocks = [blocks[i : i + 2] for i in range(0, len(blocks), 2)]
    blocks = [halves(own), *blocks, halves(samples), halves(u)]

    def body(where, x, acc):
        y = split2(x)
        stack[: y.shape[0], where] = y
        return acc + lax.dot_general(y, y, NT, preferred_element_type=F32)

    rows = ROWS * len(blocks)
    acc = column_chunks(blocks, body, jnp.zeros((2 * rows, 2 * rows), F32))
    acc = fold(acc, rows, rows)
    near, q = rows - 2 * ROWS, z.shape[0]
    z[...] = jnp.zeros(z.shape, F32)
    z[:, :near] = acc[:q, :near]
    z[: near - q, 2 * q : q + near] = acc[q:near, q:near]
    z[: 2 * ROWS, 3 * q :] = acc[near:, :q]
    z[2 * ROWS :, 3 * q : 2 * q + near] = acc[near:, q:near]


def early(samples, u, own, blocks):
    rows = ROWS * (3 + len(blocks) // 2)
    shapes = (
        jax.ShapeDtypeStruct((ROWS * RINGS // 2, 2 * ROWS * RINGS), F32),
        jax.ShapeDtypeStruct((2 * (rows + ROWS), own.shape[1]), BF),
    )
    return call(early_kernel, shapes, (own, *blocks, samples, u), 10**9, name="early")


def far_products(pieces, places, stack, acc):
    for piece, start in zip(pieces, places, strict=True):
        where = slice(start, start + piece.shape[1])
        y = split2(piece[...])
        stack[stack.shape[0] - 2 * ROWS :, where] = y
        acc = acc + lax.dot_general(y, stack[:, where], NT, preferred_element_type=F32)
    return acc


def far_kernel(places, first, second, _, acc, stack):
    acc[...] = far_products((first, second), places, stack, jnp.zeros(acc.shape, F32))


def last_kernel(places, first, second, acc, z1, _, z, stack):
    new, old = ROWS, stack.shape[0] // 2 - ROWS
    acc = far_products((first, second), places, stack, acc[...])
    left, right = fold(acc[:, : 2 * old], new, old), fold(acc[:, 2 * old :], new, new)
    near, q = old - 2 * ROWS, z.shape[0]
    column = left.T
    z[...] = z1[...]
    z[:, near : 2 * q] = column[:q]
    z[: near - q, q + near : 3 * q] = column[q:near]
    z[near - q :, 2 * q : q + near] = left[:, q:near]
    z[near - q :, q + near : 3 * q] = right
    z[2 * ROWS :, 2 * q + near :] = column[near:]


def in_place(kernel, places, shape, args, name):
    shapes = (shape, jax.ShapeDtypeStruct(args[-1].shape, BF))

    def body(*refs):
        kernel(places, *refs)

    alias = {len(args) - 1: 1}
    return call(body, shapes, args, 10**9, input_output_aliases=alias, name=name)


def last(far, z1, stack):
    quarter = far[0].shape[1]
    acc = jax.ShapeDtypeStruct((2 * ROWS, stack.shape[0]), F32)
    acc, stack = in_place(far_kernel, (0, 2 * quarter), acc, (far[0], far[2], stack), "far")
    z = jax.ShapeDtypeStruct(z1.shape, F32)
    args = (far[1], far[3], acc, z1, stack)
    return in_place(last_kernel, (quarter, 3 * quarter), z, args, "last")


def exponentials(x):
    e = jnp.exp(x - jnp.max(x, axis=1, keepdims=True))
    return e, 1.0 / jnp.sum(e, axis=1, keepdims=True)


def final_kernel(ncell, z_ref, stack, base, ab, out, buffer, sems):
    first = stack.shape[0] // 2 - 3 * ROWS
    k0, k1 = constants(0), constants(1)
    z = z_ref[0]
    for i in range(1, z_ref.shape[0]):
        z = z + z_ref[i]
    q = z.shape[0]
    corner, side, other, rest = [z[:, i * q : (i + 1) * q] for i in range(4)]
    eye = lax.broadcasted_iota(jnp.int32, (q, q), 0) == lax.broadcasted_iota(jnp.int32, (q, q), 1)
    norm = [jnp.sum(jnp.where(eye, x, 0.0), axis=0, keepdims=True) for x in (corner, other)]
    norm = jnp.concatenate(norm, axis=1)
    members = jnp.concatenate([z[:, : 2 * q], jnp.concatenate([side.T, other], axis=1)], axis=0)
    cross = jnp.concatenate([rest[: 2 * ROWS], rest[2 * ROWS :]], axis=1)

    def terms(k, cross):
        dist = k["alpha"] * k["alpha"] * norm - 2.0 * k["alpha"] * cross
        return exponentials(dist * (-1.0 / (2.0 * k["t"] * math.sqrt(ncell))))

    def dot(x, y):
        return lax.dot_general(
            x, y, NN, precision=lax.Precision.HIGHEST, preferred_element_type=F32
        )

    e0, scale0 = terms(k0, cross[:ROWS])
    e1, scale1 = terms(k1, cross[ROWS:] + k0["lift"] * dot(e0 * scale0, members))
    scale1 = k1["lift"] * scale1
    w = jnp.concatenate([e0, e1], axis=0)
    wh = w.astype(BF).astype(F32)
    w = jnp.concatenate([wh, w - wh], axis=0)
    none = jnp.zeros((4 * ROWS, 2 * ROWS), F32)
    near = jnp.concatenate([w[:, :first], none], axis=1)
    w = jnp.concatenate([near, near, w[:, first:], w[:, first:]], axis=1).astype(BF)
    pieces = sems.shape[0]
    width = out.shape[1] // pieces
    copies = []
    for i in range(pieces):
        to = slice(i * width, (i + 1) * width)
        m = lax.dot_general(w, stack[:, to], NN, preferred_element_type=F32)
        m = m[: 2 * ROWS] + m[2 * ROWS :]
        buffer[:, to] = base[:, to] + ab[:, to] * (scale0 * m[:ROWS]) + scale1 * m[ROWS:]
        copies.append(pltpu.make_async_copy(buffer.at[:, to], out.at[:, to], sems.at[i]))
        copies[-1].start()
    for copy in copies:
        copy.wait()


def final(ncell, z, stack, base, ab):
    def final(*refs):
        return final_kernel(ncell, *refs)

    shape = jax.ShapeDtypeStruct(base.shape, F32)
    scratch = [pltpu.VMEM(base.shape, F32), pltpu.SemaphoreType.DMA((4,))]
    args = (z, stack, base, ab)
    return call(final, shape, args, 10**9, scratch, out_space=pltpu.HBM, name="final")


def total(x):
    x = x + lax.ppermute(x, "core", [(0, 1), (1, 0)])
    x = jnp.broadcast_to(x[None], (lax.axis_size("x") * lax.axis_size("y"), *x.shape))
    return lax.all_to_all(x, ("x", "y"), split_axis=0, concat_axis=0, tiled=True)


def per_device(prior, samples, noise, obs_cells, obs_values, seismic_mask):
    cells = prior.shape[1]
    half = cells // 2
    ncell = cells * lax.axis_size("x") * lax.axis_size("y") * lax.axis_size("core")
    up = [(i, (i + 1) % RINGS) for i in range(RINGS)]
    down = [(i, (i - 1) % RINGS) for i in range(RINGS)]
    rising = [prior[:, :half], prior[:, half:]]
    falling = list(rising)
    blocks = []
    prec, targ = fields(obs_cells, obs_values, seismic_mask)
    for hop in range(3):
        if hop == 1:
            rising[0], prec, targ = lax.optimization_barrier((rising[0], prec, targ))
            u, base, ab = local_terms(samples, noise, prec, targ)
        if hop == 2:
            rising[0], u, base, ab = lax.optimization_barrier((rising[0], u, base, ab))
        for c in range(2):
            rising[c] = lax.ppermute(rising[c], "member", up)
            falling[c] = lax.ppermute(falling[c], "member", down)
        blocks += [*rising, *falling]
    z1, stack = early(samples, u, prior, blocks)
    quarter = half // 2
    rising[0], falling[1] = lax.optimization_barrier((rising[0], falling[1]))
    far = [
        lax.ppermute(x[:, i * quarter : (i + 1) * quarter], "member", way)
        for x, way in ((rising[0], up), (falling[1], down))
        for i in range(2)
    ]
    z, stack = last(far, z1, stack)
    z = total(z)
    return final(ncell, z, stack, base, ab)


def solution(mesh):
    mesh = jax.sharding.Mesh(mesh.devices.reshape(RINGS, 4, 4, 2), ("member", "x", "y", "core"))
    cell = ("x", "y", "core")
    in_specs = (
        P("member", cell),
        P("member", cell),
        P(None, "member", cell),
        P(None, cell),
        P(None, cell),
        P(None, cell),
    )
    return jax.shard_map(
        per_device, mesh=mesh, in_specs=in_specs, out_specs=P("member", cell), check_vma=False
    )
```

```python
import math

import jax
import jax.numpy as jnp
from jax import lax
from jax.experimental import pallas as pl
from jax.experimental.pallas import tpu as pltpu
from jax.sharding import PartitionSpec as P

STEPS = 2
RINGS = 8
ROWS = 8
BF = jnp.bfloat16
F32 = jnp.float32
NT = (((1,), (1,)), ((), ()))
NN = (((1,), (0,)), ((), ()))


def constants(step):
    t = 0.6 - 0.1 * step
    alpha = 1.0 - 0.95 * t
    drift = -0.95 / alpha
    diffusion = 1.0 - 2.0 * drift * t
    return dict(
        t=t,
        alpha=alpha,
        gain=1.0 - 0.1 * drift - 0.1 * diffusion / t,
        pull=0.1 * diffusion * (1.0 - t),
        lift=0.1 * diffusion * alpha / t,
        kick=math.sqrt(0.1 * diffusion),
    )


def split3(x):
    a = x.astype(BF).astype(F32)
    r = x - a
    b = r.astype(BF).astype(F32)
    return a, b, r - b


def fields_kernel(cells, vals, mask, prec, targ):
    width = prec.shape[0]
    obs = cells.shape[1]
    rows = lax.broadcasted_iota(jnp.int32, (width, obs), 0)
    eye = lax.broadcasted_iota(jnp.int32, (width, width), 0) == lax.broadcasted_iota(
        jnp.int32, (width, width), 1
    )
    p_sum = jnp.zeros((width, width), F32)
    t_sum = jnp.zeros((width, width), F32)
    for s in range(cells.shape[0]):
        local = cells[s : s + 1, :] & (width * width - 1)
        high = jnp.where(rows == (local >> 7), 1.0, 0.0).astype(BF)
        low = rows == (local & 127)
        pieces = [jnp.ones((1, obs), F32), *split3(vals[s : s + 1, :])]
        sums = [
            lax.dot_general(
                high, jnp.where(low, piece, 0.0).astype(BF), NT, preferred_element_type=F32
            )
            for piece in pieces
        ]
        flags = mask[s : s + 1, :].astype(F32)
        flags = jnp.sum(jnp.where(eye, flags, 0.0), axis=1, keepdims=True)
        p_sum += flags * sums[0]
        t_sum += flags * (sums[1] + sums[2] + sums[3])
    prec[...] = p_sum
    targ[...] = t_sum


def fields(*args):
    shape = jax.ShapeDtypeStruct((128, 128), F32)
    return call(fields_kernel, (shape, shape), args, 10**9, name="fields")


def per_row(prec, targ, body):
    width = prec.shape[1]

    def step(h, carry):
        where = pl.ds(pl.multiple_of(h * width, width), width)
        body(where, prec[pl.ds(h, 1), :], targ[pl.ds(h, 1), :])
        return carry

    lax.fori_loop(0, prec.shape[0], step, 0, unroll=8)


def local_kernel(samples, noise, prec, targ, u, base, ab):
    k0, k1 = constants(0), constants(1)

    def local(where, p, t):
        a1 = k1["gain"] - k1["pull"] * p
        x = (k0["gain"] - k0["pull"] * p) * samples[:, where]
        x = x + k0["pull"] * t + k0["kick"] * noise[0, :, where]
        u[:, where] = x
        base[:, where] = a1 * x + k1["pull"] * t + k1["kick"] * noise[1, :, where]
        ab[:, where] = jnp.broadcast_to(k0["lift"] * a1, x.shape)

    per_row(prec, targ, local)


def local_terms(*args):
    shape = jax.ShapeDtypeStruct(args[0].shape, F32)
    return call(local_kernel, (shape, shape, shape), args, 10**9, name="local")


CHUNK = 4096
LIMIT = pltpu.CompilerParams(vmem_limit_bytes=16 << 20)


def call(kernel, out_shape, args, flops, scratch=(), space=pltpu.VMEM, out_space=pltpu.VMEM, **kw):
    out_spec = pl.BlockSpec(memory_space=out_space)
    return pl.pallas_call(
        kernel,
        out_shape=out_shape,
        in_specs=[pl.BlockSpec(memory_space=space)] * len(args),
        out_specs=jax.tree.map(lambda _: out_spec, out_shape),
        scratch_shapes=scratch,
        compiler_params=LIMIT,
        cost_estimate=pl.CostEstimate(flops=flops, bytes_accessed=4 * 10**6, transcendentals=0),
        **kw,
    )(*args)


def split2(x):
    high = x.astype(BF).astype(F32)
    return jnp.concatenate([high, x - high], axis=0).astype(BF)


def column_chunks(blocks, body, acc):
    done = 0
    for pieces in zip(*blocks, strict=True):
        width = pieces[0].shape[1]
        for start in range(0, width, CHUNK):
            x = jnp.concatenate([p[:, start : start + CHUNK] for p in pieces], axis=0)
            acc = body(slice(done + start, done + start + CHUNK), x, acc)
        done += width
    return acc


def halves(full):
    half = full.shape[1] // 2
    return [full.at[:, :half], full.at[:, half:]]


def fold(z, m, n):
    z = z[:m] + z[m:]
    return z[:, :n] + z[:, n:]


def early_kernel(own, *refs):
    blocks, samples, u, z, stack = refs[:-4], *refs[-4:]
    blocks = [blocks[i : i + 2] for i in range(0, len(blocks), 2)]
    blocks = [halves(own), *blocks, halves(samples), halves(u)]

    def body(where, x, acc):
        y = split2(x)
        stack[: y.shape[0], where] = y
        return acc + lax.dot_general(y, y, NT, preferred_element_type=F32)

    rows = ROWS * len(blocks)
    acc = column_chunks(blocks, body, jnp.zeros((2 * rows, 2 * rows), F32))
    acc = fold(acc, rows, rows)
    near, q = rows - 2 * ROWS, z.shape[0]
    z[...] = jnp.zeros(z.shape, F32)
    z[:, :near] = acc[:q, :near]
    z[: near - q, 2 * q : q + near] = acc[q:near, q:near]
    z[: 2 * ROWS, 3 * q :] = acc[near:, :q]
    z[2 * ROWS :, 3 * q : 2 * q + near] = acc[near:, q:near]


def early(samples, u, own, blocks):
    rows = ROWS * (3 + len(blocks) // 2)
    shapes = (
        jax.ShapeDtypeStruct((ROWS * RINGS // 2, 2 * ROWS * RINGS), F32),
        jax.ShapeDtypeStruct((2 * (rows + ROWS), own.shape[1]), BF),
    )
    return call(early_kernel, shapes, (own, *blocks, samples, u), 10**9, name="early")


def last_kernel(*refs):
    far, z1, _, z, stack = refs[:-4], *refs[-4:]
    new, old = ROWS, stack.shape[0] // 2 - ROWS

    def body(where, x, acc):
        y = split2(x)
        stack[2 * old :, where] = y
        return acc + lax.dot_general(y, stack[:, where], NT, preferred_element_type=F32)

    acc = column_chunks([far], body, jnp.zeros((2 * new, 2 * (old + new)), F32))
    left, right = fold(acc[:, : 2 * old], new, old), fold(acc[:, 2 * old :], new, new)
    near, q = old - 2 * ROWS, z.shape[0]
    column = left.T
    z[...] = z1[...]
    z[:, near : 2 * q] = column[:q]
    z[: near - q, q + near : 3 * q] = column[q:near]
    z[near - q :, 2 * q : q + near] = left[:, q:near]
    z[near - q :, q + near : 3 * q] = right
    z[2 * ROWS :, 2 * q + near :] = column[near:]


def last(far, z1, stack):
    shapes = (jax.ShapeDtypeStruct(z1.shape, F32), jax.ShapeDtypeStruct(stack.shape, BF))
    args = (*far, z1, stack)
    places = {len(args) - 1: 1}
    return call(last_kernel, shapes, args, 10**9, input_output_aliases=places, name="last")


def exponentials(x):
    e = jnp.exp(x - jnp.max(x, axis=1, keepdims=True))
    return e, 1.0 / jnp.sum(e, axis=1, keepdims=True)


def final_kernel(ncell, z_ref, stack, base, ab, out, buffer, sems):
    first = stack.shape[0] // 2 - 3 * ROWS
    k0, k1 = constants(0), constants(1)
    z = z_ref[0]
    for i in range(1, z_ref.shape[0]):
        z = z + z_ref[i]
    q = z.shape[0]
    corner, side, other, rest = [z[:, i * q : (i + 1) * q] for i in range(4)]
    eye = lax.broadcasted_iota(jnp.int32, (q, q), 0) == lax.broadcasted_iota(jnp.int32, (q, q), 1)
    norm = [jnp.sum(jnp.where(eye, x, 0.0), axis=0, keepdims=True) for x in (corner, other)]
    norm = jnp.concatenate(norm, axis=1)
    members = jnp.concatenate([z[:, : 2 * q], jnp.concatenate([side.T, other], axis=1)], axis=0)
    cross = jnp.concatenate([rest[: 2 * ROWS], rest[2 * ROWS :]], axis=1)

    def terms(k, cross):
        dist = k["alpha"] * k["alpha"] * norm - 2.0 * k["alpha"] * cross
        return exponentials(dist * (-1.0 / (2.0 * k["t"] * math.sqrt(ncell))))

    def dot(x, y):
        return lax.dot_general(
            x, y, NN, precision=lax.Precision.HIGHEST, preferred_element_type=F32
        )

    e0, scale0 = terms(k0, cross[:ROWS])
    e1, scale1 = terms(k1, cross[ROWS:] + k0["lift"] * dot(e0 * scale0, members))
    scale1 = k1["lift"] * scale1
    w = jnp.concatenate([e0, e1], axis=0)
    wh = w.astype(BF).astype(F32)
    w = jnp.concatenate([wh, w - wh], axis=0)
    none = jnp.zeros((4 * ROWS, 2 * ROWS), F32)
    near = jnp.concatenate([w[:, :first], none], axis=1)
    w = jnp.concatenate([near, near, w[:, first:], w[:, first:]], axis=1).astype(BF)
    pieces = sems.shape[0]
    width = out.shape[1] // pieces
    copies = []
    for i in range(pieces):
        to = slice(i * width, (i + 1) * width)
        m = lax.dot_general(w, stack[:, to], NN, preferred_element_type=F32)
        m = m[: 2 * ROWS] + m[2 * ROWS :]
        buffer[:, to] = base[:, to] + ab[:, to] * (scale0 * m[:ROWS]) + scale1 * m[ROWS:]
        copies.append(pltpu.make_async_copy(buffer.at[:, to], out.at[:, to], sems.at[i]))
        copies[-1].start()
    for copy in copies:
        copy.wait()


def final(ncell, z, stack, base, ab):
    def final(*refs):
        return final_kernel(ncell, *refs)

    shape = jax.ShapeDtypeStruct(base.shape, F32)
    scratch = [pltpu.VMEM(base.shape, F32), pltpu.SemaphoreType.DMA((4,))]
    args = (z, stack, base, ab)
    return call(final, shape, args, 10**9, scratch, out_space=pltpu.HBM, name="final")


def total(x):
    x = x + lax.ppermute(x, "core", [(0, 1), (1, 0)])
    x = jnp.broadcast_to(x[None], (lax.axis_size("x") * lax.axis_size("y"), *x.shape))
    return lax.all_to_all(x, ("x", "y"), split_axis=0, concat_axis=0, tiled=True)


def per_device(prior, samples, noise, obs_cells, obs_values, seismic_mask):
    cells = prior.shape[1]
    half = cells // 2
    ncell = cells * lax.axis_size("x") * lax.axis_size("y") * lax.axis_size("core")
    up = [(i, (i + 1) % RINGS) for i in range(RINGS)]
    down = [(i, (i - 1) % RINGS) for i in range(RINGS)]
    rising = [prior[:, :half], prior[:, half:]]
    falling = list(rising)
    blocks = []
    prec, targ = fields(obs_cells, obs_values, seismic_mask)
    for hop in range(3):
        if hop == 1:
            rising[0], prec, targ = lax.optimization_barrier((rising[0], prec, targ))
            u, base, ab = local_terms(samples, noise, prec, targ)
        if hop == 2:
            rising[0], u, base, ab = lax.optimization_barrier((rising[0], u, base, ab))
        for c in range(2):
            rising[c] = lax.ppermute(rising[c], "member", up)
            falling[c] = lax.ppermute(falling[c], "member", down)
        blocks += [*rising, *falling]
    z1, stack = early(samples, u, prior, blocks)
    far = [lax.ppermute(rising[0], "member", up), lax.ppermute(falling[1], "member", down)]
    z, stack = last(far, z1, stack)
    z = total(z)
    return final(ncell, z, stack, base, ab)


def solution(mesh):
    mesh = jax.sharding.Mesh(mesh.devices.reshape(RINGS, 4, 4, 2), ("member", "x", "y", "core"))
    cell = ("x", "y", "core")
    in_specs = (
        P("member", cell),
        P("member", cell),
        P(None, "member", cell),
        P(None, cell),
        P(None, cell),
        P(None, cell),
    )
    return jax.shard_map(
        per_device, mesh=mesh, in_specs=in_specs, out_specs=P("member", cell), check_vma=False
    )
```

```python
import math

import jax
import jax.numpy as jnp
from jax import lax
from jax.experimental import pallas as pl
from jax.experimental.pallas import tpu as pltpu
from jax.sharding import PartitionSpec as P

STEPS = 2
RINGS = 8
ROWS = 8
BF = jnp.bfloat16
F32 = jnp.float32
NT = (((1,), (1,)), ((), ()))
NN = (((1,), (0,)), ((), ()))


def constants(step):
    t = 0.6 - 0.1 * step
    alpha = 1.0 - 0.95 * t
    drift = -0.95 / alpha
    diffusion = 1.0 - 2.0 * drift * t
    return dict(
        t=t,
        alpha=alpha,
        gain=1.0 - 0.1 * drift - 0.1 * diffusion / t,
        pull=0.1 * diffusion * (1.0 - t),
        lift=0.1 * diffusion * alpha / t,
        kick=math.sqrt(0.1 * diffusion),
    )


def split3(x):
    a = x.astype(BF).astype(F32)
    r = x - a
    b = r.astype(BF).astype(F32)
    return a, b, r - b


def fields_kernel(cells, vals, mask, prec, targ):
    width = prec.shape[0]
    obs = cells.shape[1]
    rows = lax.broadcasted_iota(jnp.int32, (width, obs), 0)
    eye = lax.broadcasted_iota(jnp.int32, (width, width), 0) == lax.broadcasted_iota(
        jnp.int32, (width, width), 1
    )
    p_sum = jnp.zeros((width, width), F32)
    t_sum = jnp.zeros((width, width), F32)
    for s in range(cells.shape[0]):
        local = cells[s : s + 1, :] & (width * width - 1)
        high = jnp.where(rows == (local >> 7), 1.0, 0.0).astype(BF)
        low = rows == (local & 127)
        pieces = [jnp.ones((1, obs), F32), *split3(vals[s : s + 1, :])]
        sums = [
            lax.dot_general(
                high, jnp.where(low, piece, 0.0).astype(BF), NT, preferred_element_type=F32
            )
            for piece in pieces
        ]
        flags = mask[s : s + 1, :].astype(F32)
        flags = jnp.sum(jnp.where(eye, flags, 0.0), axis=1, keepdims=True)
        p_sum += flags * sums[0]
        t_sum += flags * (sums[1] + sums[2] + sums[3])
    prec[...] = p_sum
    targ[...] = t_sum


def fields(*args):
    shape = jax.ShapeDtypeStruct((128, 128), F32)
    return call(fields_kernel, (shape, shape), args, 10**9, name="fields")


def per_row(prec, targ, body):
    width = prec.shape[1]

    def step(h, carry):
        where = pl.ds(pl.multiple_of(h * width, width), width)
        body(where, prec[pl.ds(h, 1), :], targ[pl.ds(h, 1), :])
        return carry

    lax.fori_loop(0, prec.shape[0], step, 0, unroll=8)


def local_kernel(samples, noise, prec, targ, u, base, ab):
    k0, k1 = constants(0), constants(1)

    def local(where, p, t):
        a1 = k1["gain"] - k1["pull"] * p
        x = (k0["gain"] - k0["pull"] * p) * samples[:, where]
        x = x + k0["pull"] * t + k0["kick"] * noise[0, :, where]
        u[:, where] = x
        base[:, where] = a1 * x + k1["pull"] * t + k1["kick"] * noise[1, :, where]
        ab[:, where] = jnp.broadcast_to(k0["lift"] * a1, x.shape)

    per_row(prec, targ, local)


def local_terms(*args):
    shape = jax.ShapeDtypeStruct(args[0].shape, F32)
    return call(local_kernel, (shape, shape, shape), args, 10**9, name="local")


CHUNK = 8192
LIMIT = pltpu.CompilerParams(vmem_limit_bytes=16 << 20)


def call(kernel, out_shape, args, flops, scratch=(), space=pltpu.VMEM, out_space=pltpu.VMEM, **kw):
    out_spec = pl.BlockSpec(memory_space=out_space)
    return pl.pallas_call(
        kernel,
        out_shape=out_shape,
        in_specs=[pl.BlockSpec(memory_space=space)] * len(args),
        out_specs=jax.tree.map(lambda _: out_spec, out_shape),
        scratch_shapes=scratch,
        compiler_params=LIMIT,
        cost_estimate=pl.CostEstimate(flops=flops, bytes_accessed=4 * 10**6, transcendentals=0),
        **kw,
    )(*args)


def split2(x):
    high = x.astype(BF).astype(F32)
    return jnp.concatenate([high, x - high], axis=0).astype(BF)


def column_chunks(blocks, body, acc):
    done = 0
    for pieces in zip(*blocks, strict=True):
        width = pieces[0].shape[1]
        for start in range(0, width, CHUNK):
            x = jnp.concatenate([p[:, start : start + CHUNK] for p in pieces], axis=0)
            acc = body(slice(done + start, done + start + CHUNK), x, acc)
        done += width
    return acc


def halves(full):
    half = full.shape[1] // 2
    return [full.at[:, :half], full.at[:, half:]]


def fold(z, m, n):
    z = z[:m] + z[m:]
    return z[:, :n] + z[:, n:]


def early_kernel(own, *refs):
    blocks, samples, u, z, stack = refs[:-4], *refs[-4:]
    blocks = [blocks[i : i + 2] for i in range(0, len(blocks), 2)]
    blocks = [halves(own), *blocks, halves(samples), halves(u)]

    def body(where, x, acc):
        y = split2(x)
        stack[: y.shape[0], where] = y
        return acc + lax.dot_general(y, y, NT, preferred_element_type=F32)

    rows = ROWS * len(blocks)
    acc = column_chunks(blocks, body, jnp.zeros((2 * rows, 2 * rows), F32))
    acc = fold(acc, rows, rows)
    near, q = rows - 2 * ROWS, z.shape[0]
    z[...] = jnp.zeros(z.shape, F32)
    z[:, :near] = acc[:q, :near]
    z[: near - q, 2 * q : q + near] = acc[q:near, q:near]
    z[: 2 * ROWS, 3 * q :] = acc[near:, :q]
    z[2 * ROWS :, 3 * q : 2 * q + near] = acc[near:, q:near]


def early(samples, u, own, blocks):
    rows = ROWS * (3 + len(blocks) // 2)
    shapes = (
        jax.ShapeDtypeStruct((ROWS * RINGS // 2, 2 * ROWS * RINGS), F32),
        jax.ShapeDtypeStruct((2 * (rows + ROWS), own.shape[1]), BF),
    )
    return call(early_kernel, shapes, (own, *blocks, samples, u), 10**9, name="early")


def last_kernel(*refs):
    far, z1, _, z, stack = refs[:-4], *refs[-4:]
    new, old = ROWS, stack.shape[0] // 2 - ROWS

    def body(where, x, acc):
        y = split2(x)
        stack[2 * old :, where] = y
        return acc + lax.dot_general(y, stack[:, where], NT, preferred_element_type=F32)

    acc = column_chunks([far], body, jnp.zeros((2 * new, 2 * (old + new)), F32))
    left, right = fold(acc[:, : 2 * old], new, old), fold(acc[:, 2 * old :], new, new)
    near, q = old - 2 * ROWS, z.shape[0]
    column = left.T
    z[...] = z1[...]
    z[:, near : 2 * q] = column[:q]
    z[: near - q, q + near : 3 * q] = column[q:near]
    z[near - q :, 2 * q : q + near] = left[:, q:near]
    z[near - q :, q + near : 3 * q] = right
    z[2 * ROWS :, 2 * q + near :] = column[near:]


def last(far, z1, stack):
    shapes = (jax.ShapeDtypeStruct(z1.shape, F32), jax.ShapeDtypeStruct(stack.shape, BF))
    args = (*far, z1, stack)
    places = {len(args) - 1: 1}
    return call(last_kernel, shapes, args, 10**9, input_output_aliases=places, name="last")


def exponentials(x):
    e = jnp.exp(x - jnp.max(x, axis=1, keepdims=True))
    return e, 1.0 / jnp.sum(e, axis=1, keepdims=True)


def final_kernel(ncell, z_ref, stack, base, ab, out, buffer, sems):
    first = stack.shape[0] // 2 - 3 * ROWS
    k0, k1 = constants(0), constants(1)
    z = z_ref[0]
    for i in range(1, z_ref.shape[0]):
        z = z + z_ref[i]
    q = z.shape[0]
    corner, side, other, rest = [z[:, i * q : (i + 1) * q] for i in range(4)]
    eye = lax.broadcasted_iota(jnp.int32, (q, q), 0) == lax.broadcasted_iota(jnp.int32, (q, q), 1)
    norm = [jnp.sum(jnp.where(eye, x, 0.0), axis=0, keepdims=True) for x in (corner, other)]
    norm = jnp.concatenate(norm, axis=1)
    members = jnp.concatenate([z[:, : 2 * q], jnp.concatenate([side.T, other], axis=1)], axis=0)
    cross = jnp.concatenate([rest[: 2 * ROWS], rest[2 * ROWS :]], axis=1)

    def terms(k, cross):
        dist = k["alpha"] * k["alpha"] * norm - 2.0 * k["alpha"] * cross
        return exponentials(dist * (-1.0 / (2.0 * k["t"] * math.sqrt(ncell))))

    def dot(x, y):
        return lax.dot_general(
            x, y, NN, precision=lax.Precision.HIGHEST, preferred_element_type=F32
        )

    e0, scale0 = terms(k0, cross[:ROWS])
    e1, scale1 = terms(k1, cross[ROWS:] + k0["lift"] * dot(e0 * scale0, members))
    scale1 = k1["lift"] * scale1
    w = jnp.concatenate([e0, e1], axis=0)
    wh = w.astype(BF).astype(F32)
    w = jnp.concatenate([wh, w - wh], axis=0)
    none = jnp.zeros((4 * ROWS, 2 * ROWS), F32)
    near = jnp.concatenate([w[:, :first], none], axis=1)
    w = jnp.concatenate([near, near, w[:, first:], w[:, first:]], axis=1).astype(BF)
    pieces = sems.shape[0]
    width = out.shape[1] // pieces
    copies = []
    for i in range(pieces):
        to = slice(i * width, (i + 1) * width)
        m = lax.dot_general(w, stack[:, to], NN, preferred_element_type=F32)
        m = m[: 2 * ROWS] + m[2 * ROWS :]
        buffer[:, to] = base[:, to] + ab[:, to] * (scale0 * m[:ROWS]) + scale1 * m[ROWS:]
        copies.append(pltpu.make_async_copy(buffer.at[:, to], out.at[:, to], sems.at[i]))
        copies[-1].start()
    for copy in copies:
        copy.wait()


def final(ncell, z, stack, base, ab):
    def final(*refs):
        return final_kernel(ncell, *refs)

    shape = jax.ShapeDtypeStruct(base.shape, F32)
    scratch = [pltpu.VMEM(base.shape, F32), pltpu.SemaphoreType.DMA((4,))]
    args = (z, stack, base, ab)
    return call(final, shape, args, 10**9, scratch, out_space=pltpu.HBM, name="final")


def total(x):
    x = x + lax.ppermute(x, "core", [(0, 1), (1, 0)])
    x = jnp.broadcast_to(x[None], (lax.axis_size("x") * lax.axis_size("y"), *x.shape))
    return lax.all_to_all(x, ("x", "y"), split_axis=0, concat_axis=0, tiled=True)


def per_device(prior, samples, noise, obs_cells, obs_values, seismic_mask):
    cells = prior.shape[1]
    half = cells // 2
    ncell = cells * lax.axis_size("x") * lax.axis_size("y") * lax.axis_size("core")
    up = [(i, (i + 1) % RINGS) for i in range(RINGS)]
    down = [(i, (i - 1) % RINGS) for i in range(RINGS)]
    rising = [prior[:, :half], prior[:, half:]]
    falling = list(rising)
    blocks = []
    prec, targ = fields(obs_cells, obs_values, seismic_mask)
    for hop in range(3):
        if hop == 1:
            rising[0], prec, targ = lax.optimization_barrier((rising[0], prec, targ))
            u, base, ab = local_terms(samples, noise, prec, targ)
        if hop == 2:
            rising[0], u, base, ab = lax.optimization_barrier((rising[0], u, base, ab))
        for c in range(2):
            rising[c] = lax.ppermute(rising[c], "member", up)
            falling[c] = lax.ppermute(falling[c], "member", down)
        blocks += [*rising, *falling]
    z1, stack = early(samples, u, prior, blocks)
    far = [lax.ppermute(rising[0], "member", up), lax.ppermute(falling[1], "member", down)]
    z, stack = last(far, z1, stack)
    z = total(z)
    return final(ncell, z, stack, base, ab)


def solution(mesh):
    mesh = jax.sharding.Mesh(mesh.devices.reshape(RINGS, 4, 4, 2), ("member", "x", "y", "core"))
    cell = ("x", "y", "core")
    in_specs = (
        P("member", cell),
        P("member", cell),
        P(None, "member", cell),
        P(None, cell),
        P(None, cell),
        P(None, cell),
    )
    return jax.shard_map(
        per_device, mesh=mesh, in_specs=in_specs, out_specs=P("member", cell), check_vma=False
    )
```
